128 devices in a mesh: ctx: 4 (over y), ch: 32 (over z, x, core).
Axes of the slice: x: 4, y: 4, z: 4, core: 2. Of those that a mesh axis runs over, the one named last changes fastest.
Arguments:
- streams: bfloat16 [16384, 3, 8192], P(('ctx', 'ch')), may hold values from -6 to 6
- load_counts: int32 [4, 32], P('ctx'), may hold values from 1 to 128, 2048 in all within a row
- seg_ids: int32 [8192], P('ctx'), may hold values from 0 to 3, never falling along the last dimension, each value on 1 to 4096 neighbouring positions
- rates: float32 [8192, 16], P('ch'), may hold values from 1.2207031e-05 to 0.05
- residues: float32 [8192, 16], P('ch'), may hold values from -1.5 to 1.5
- skip: float32 [8192], P('ch'), may hold values from 0.5 to 1.5
Outputs:
- mixed: bfloat16 [8192, 8192], P('ctx', 'ch')
The draws below stay inside these ranges and needn't reach their ends.
Inputs may be any that keep to these rules, and one draw needn't show every extreme that they name: `load_counts`: each row sums to 2048 and its largest entry equals 128. `seg_ids`: never falls; each segment holds 1 to 4096 positions, one exactly that many.
All inputs are finite; a program needn't handle non-finite values.
Results may differ from the reference program's by a relative error of at most 0.0049.
Values may be sent and summed in bfloat16 or wider, within the bound.
No kernel may reach another device: no remote copies, remote signals or barrier semaphores. Data moves between devices by JAX's collectives and lax.ppermute only.
A program may use at most 192 MiB of HBM per device.

```python
import math
import jax
import jax.numpy as jnp
import numpy as np
from jax import lax

ORDER = 16
L_DEV = 2048
SEGS = 4
D = 8192
SEQ = 8192
LOAD_CAP = 128
N_CTX = 4
N_CH = 32


def draw_rates(key, part):
    key_slow, key_level = jax.random.split(key, 2)
    slow = jax.random.bernoulli(key_slow, 0.5, (D, ORDER))
    level = jax.random.uniform(key_level, (D, ORDER), jnp.float32)
    low_rate = 0.1 / SEQ
    mid_rate = 1.0 / SEQ
    slow_rate = low_rate * (mid_rate / low_rate) ** level
    fast_rate = mid_rate * (0.05 / mid_rate) ** level
    return jnp.where(slow, slow_rate, fast_rate).astype(jnp.float32)


def levels(rng, shape, cuts, smallest, high):
    factor_of = 1.0
    for dim, blocks in cuts:
        draws = jax.random.uniform(jax.random.fold_in(jax.random.fold_in(rng, 6), dim), (blocks,), jnp.float32, smallest / len(cuts), high / len(cuts))
        factor_of = factor_of * jnp.repeat(jnp.exp(draws), shape[dim] // blocks).reshape((-1,) + (1,) * (len(shape) - 1 - dim))
    return factor_of


def split_up(count, total, bound, skew):
    portions = [(1 << 20) // math.isqrt(rank ** skew) + 1 for rank in range(2, count + 1)]
    surplus, given = total - bound - (count - 1), [1] * (count - 1)
    while surplus > 0:
        movable = [i for i in range(count - 1) if given[i] < bound]
        mass, left = sum([portions[i] for i in movable]), surplus
        for i in movable:
            extra = min(bound - given[i], max(1, left * portions[i] // mass), surplus)
            given[i] = given[i] + extra
            surplus = surplus - extra
    return np.array([bound] + given)


def ragged(key, number_of, total, reach, skew):
    if number_of == 2:
        one = jax.random.randint(key, (), max(1, total - reach), min(reach, total - 1) + 1)
        return jnp.stack([one, total - one])
    tallies = jnp.asarray(split_up(number_of, total, reach, skew), jnp.int32)
    twos = (number_of - 1) // 2
    giver, sink = tallies[1:1 + 2 * twos:2], tallies[2:2 + 2 * twos:2]
    slack = jnp.minimum(giver - 1, reach - sink)
    moved = jax.random.randint(jax.random.fold_in(key, 1), (twos,), 0, 1 << 20) % (slack + 1)
    tallies = tallies.at[1:1 + 2 * twos:2].set(giver - moved).at[2:2 + 2 * twos:2].set(sink + moved)
    return tallies[jax.random.permutation(jax.random.fold_in(key, 2), number_of)]


def bell_draw(own_key, extent, scale, most, cuts=(), held_as=jnp.bfloat16):
    level = levels(own_key, extent, cuts, -0.22, 0.18) if cuts else 1.0
    values = jax.random.normal(own_key, extent, jnp.float32) * scale * level
    return jnp.minimum(jnp.maximum(values, -most), most).astype(held_as)


def setup_inputs(seed: int = 0) -> dict:
    key_list = jax.random.split(jax.random.key(seed), 7)
    return {
        "streams": bell_draw(key_list[0], (N_CTX * N_CH * LOAD_CAP, 3, D), 1.0, 6.0, ((0, 128),)),
        "load_counts": jax.vmap(lambda own: ragged(own, N_CH, L_DEV, LOAD_CAP, 2))(jax.random.split(key_list[1], N_CTX)).reshape((N_CTX, N_CH)).astype(jnp.int32),
        "seg_ids": jnp.searchsorted(jnp.cumsum(ragged(key_list[2], SEGS, SEQ, SEQ // 2, 1)), jnp.arange(SEQ), side="right").astype(jnp.int32),
        "rates": draw_rates(jax.random.fold_in(key_list[6], 71), 0),
        "residues": bell_draw(key_list[4], (D, ORDER), ORDER ** -0.5, 1.5, ((0, 32),), jnp.float32),
        "skip": jnp.clip(0.5 + 1.0 * jax.random.uniform(key_list[5], (D,), jnp.float32) ** levels(key_list[5], (D,), ((0, 32),), -0.2, 0.2), 0.5, 1.5),
    }


def reference(streams, load_counts, seg_ids, rates, residues, skip):
    loaded = streams.reshape(N_CTX, N_CH, LOAD_CAP, 3, D)
    position = jnp.arange(L_DEV, dtype=jnp.int32)
    ending = jnp.cumsum(load_counts, axis=1).astype(jnp.int32)
    passed = ending[:, None, :] <= position[None, :, None]
    source = lax.optimization_barrier(jnp.sum(passed.astype(jnp.int32), axis=2)).astype(jnp.int32)
    starts = lax.optimization_barrier(jnp.sum(jnp.where(passed, load_counts[:, None, :], 0), axis=2)).astype(jnp.int32)
    slot_index = (position[None, :] - starts).astype(jnp.int32)
    span_ids = jnp.broadcast_to(jnp.arange(N_CTX, dtype=jnp.int32)[:, None], (N_CTX, L_DEV))
    placed = loaded[span_ids, source, slot_index].reshape(SEQ, 3, D)
    query = placed[:, 0]
    signal = (placed[:, 1].astype(jnp.float32) * placed[:, 2].astype(jnp.float32)).astype(jnp.bfloat16)
    decay = jnp.exp(-rates)
    gain = jnp.sqrt(-jnp.expm1(-2.0 * rates))
    keep = jnp.concatenate([jnp.zeros((1,), jnp.float32), (seg_ids[1:] == seg_ids[:-1]).astype(jnp.float32)])

    def advance(state, inputs):
        signal_row, keep_row = inputs
        state = keep_row * decay * state + gain * signal_row[:, None]
        return (state, lax.optimization_barrier(jnp.sum(residues * state, axis=1)))
    _, conv = lax.scan(advance, jnp.zeros((D, ORDER), jnp.float32), (signal.astype(jnp.float32), keep))
    mixed = query.astype(jnp.float32) * (conv + skip[None, :] * signal.astype(jnp.float32))
    return mixed.astype(jnp.bfloat16)
```

```python
import functools

import jax
import jax.numpy as jnp
from jax import lax
from jax.experimental import pallas as pl
from jax.experimental.pallas import tpu as pltpu
from jax.sharding import PartitionSpec as P

BLOCK = 128
STEPS = 16
LANES = 128
SUB = 8
F32 = jnp.float32
BF16 = jnp.bfloat16


def slot_position(shape, dim):
    slot = lax.broadcasted_iota(jnp.int32, shape, dim)
    return (slot & (SUB - 1)) * STEPS + (slot >> 3)


def rotation(shift):
    place = slot_position((BLOCK, BLOCK), 0)
    row = lax.broadcasted_iota(jnp.int32, (BLOCK, BLOCK), 1)
    return jnp.where(((row + shift) & (BLOCK - 1)) == place, 1.0, 0.0).astype(BF16)


def send_signal_kernel(shift, key_ref, value_ref, out_ref):
    turn = rotation(shift[0])
    signal = (key_ref[0].astype(F32) * value_ref[0].astype(F32)).astype(BF16)
    moved = jnp.dot(turn, signal, preferred_element_type=F32).astype(BF16)
    channels = out_ref.shape[2]
    for part in range(out_ref.shape[0]):
        out_ref[part] = moved[:, part * channels : (part + 1) * channels]


def send_query_kernel(shift, query_ref, out_ref):
    turn = rotation(shift[0])
    moved = jnp.dot(turn, query_ref[0], preferred_element_type=F32).astype(BF16)
    channels = out_ref.shape[2]
    for part in range(out_ref.shape[0]):
        out_ref[part] = moved[:, part * channels : (part + 1) * channels]


def send(kernel, planes, streams, shift, groups, channels, step):
    rows = streams.shape[1]
    return pl.pallas_call(
        kernel,
        out_shape=jax.ShapeDtypeStruct((groups, rows, channels), BF16),
        grid_spec=pltpu.PrefetchScalarGridSpec(
            num_scalar_prefetch=1,
            grid=(groups // step,),
            in_specs=[
                pl.BlockSpec((1, rows, step * channels), functools.partial(lambda plane, i, s: (plane, 0, i), plane))
                for plane in planes
            ],
            out_specs=pl.BlockSpec((step, rows, channels), lambda i, s: (i, 0, 0)),
        ),
    )(shift, *[streams for _ in planes])


def segment(position, bounds):
    total = (position >= bounds[0]).astype(jnp.int32)
    for bound in bounds[1:]:
        total = total + (position >= bound).astype(jnp.int32)
    return total


def gather_block(block, starts, first, last, arrived_ref, into_ref):
    place = slot_position(into_ref.shape, 0)

    def add(source, carry):
        low = starts[source] - block * BLOCK
        high = starts[source + 1] - block * BLOCK
        here = (place >= low) & (place < high)
        into_ref[...] = jnp.where(here, arrived_ref[source].astype(F32), into_ref[...])
        return carry

    lax.fori_loop(first[block], last[block], add, 0)


def scan_kernel(per, starts, first, last, bounds, arrived_ref, decay_ref, weight_ref, leap_ref, signal_ref, ends_ref, final_ref, held, carry):
    step = pl.program_id(0)
    limits = [bounds[k] for k in range(3)]
    modes = decay_ref.shape[0]
    channels = decay_ref.shape[2]

    @pl.when(step == 0)
    def _():
        carry[...] = jnp.zeros_like(carry)

    def one(inner, unused):
        block = step * per + inner
        begin = block * BLOCK
        gather_block(block, starts, first, last, arrived_ref, held)
        signal_ref[pl.ds(inner * BLOCK, BLOCK), :] = held[...].astype(BF16)
        first_id = segment(begin, limits)
        last_id = segment(begin + BLOCK - 1, limits)
        before_id = segment(begin - 1, limits)

        @pl.when(first_id != last_id)
        def _():
            place = slot_position(held.shape, 0)
            own = segment(begin + place, limits)
            end = segment(begin + (place | (STEPS - 1)), limits)
            held[...] = jnp.where(own == end, held[...], 0.0)

        rank = lax.broadcasted_iota(jnp.int32, (SUB, LANES), 0)
        reach = segment(begin + rank * STEPS + STEPS - 1, limits) == last_id
        going = jnp.where(before_id == last_id, 1.0, 0.0)
        for tile in range(channels // LANES):
            lanes = pl.ds(tile * LANES, LANES)
            rows = [held[pl.ds(t * SUB, SUB), lanes] for t in range(STEPS)]
            for mode in range(modes):
                decay = decay_ref[mode, :, lanes]
                state = rows[0]
                for t in range(1, STEPS):
                    state = decay * state + rows[t]
                ends_ref[inner, mode, :, lanes] = state
                kept = jnp.where(reach, weight_ref[mode, :, lanes] * state, 0.0)
                carry[mode, :, lanes] = (going * leap_ref[mode, :, lanes]) * carry[mode, :, lanes] + kept
        return unused

    lax.fori_loop(0, per, one, 0)

    @pl.when(step == pl.num_programs(0) - 1)
    def _():
        final_ref[...] = jnp.sum(carry[...], axis=1)


def conv_kernel(
    per, bounds, signal_ref, ends_ref, near_ref, far_ref, farther_ref, decay_ref, one_ref, two_ref, four_ref, onward_ref, scale_ref, taps_ref, span_ref, out_ref, state
):
    step = pl.program_id(0)
    limits = [bounds[k] for k in range(3)]
    modes = decay_ref.shape[0]
    channels = decay_ref.shape[2]

    @pl.when(step == 0)
    def _():
        start_id = segment(0, limits).astype(F32)
        span = span_ref[...]

        def ids(ref):
            return ref[modes : modes + 1, :], ref[modes + 1 : modes + 2, :]

        near_first, near_last = ids(near_ref)
        far_first, far_last = ids(far_ref)
        farther_first, farther_last = ids(farther_ref)
        through_far = jnp.where((far_first == far_last) & (far_first == farther_last), 1.0, 0.0)
        through_near = jnp.where((near_first == near_last) & (near_first == far_last), 1.0, 0.0)
        entering = jnp.where(near_last == start_id, 1.0, 0.0)
        inside = far_ref[0:modes, :] + through_far * span * farther_ref[0:modes, :]
        inside = near_ref[0:modes, :] + through_near * span * inside
        inside = entering * inside
        for mode in range(modes):
            state[mode] = jnp.broadcast_to(inside[mode : mode + 1], (SUB, channels))

    rank = lax.broadcasted_iota(jnp.int32, (SUB, LANES), 0)

    def one(inner, unused):
        block = step * per + inner
        begin = block * BLOCK
        last_id = segment(begin + BLOCK - 1, limits)
        before_id = segment(jnp.maximum(begin - 1, 0), limits)
        edge = segment(begin + rank * STEPS + STEPS - 1, limits)
        single = before_id == last_id

        def tiles(masked):
            if masked:
                one_in = jnp.where((rank >= 1) & (edge == pltpu.roll(edge, 1, 0)), 1.0, 0.0)
                two_in = jnp.where((rank >= 2) & (edge == pltpu.roll(edge, 2, 0)), 1.0, 0.0)
                four_in = jnp.where((rank >= 4) & (edge == pltpu.roll(edge, 4, 0)), 1.0, 0.0)
                start_in = jnp.where(edge == before_id, 1.0, 0.0)
                prior = jnp.where(rank == 0, before_id, pltpu.roll(edge, 1, 0))
                own = [segment(begin + rank * STEPS + t, limits) for t in range(STEPS)]
                open_in = [jnp.where(o == prior, 1.0, 0.0) for o in own]
            for tile in range(channels // LANES):
                lanes = pl.ds(tile * LANES, LANES)
                rows = [
                    signal_ref[pl.ds(inner * BLOCK + t * SUB, SUB), lanes].astype(F32) for t in range(STEPS)
                ]
                local = []
                for t in range(STEPS):
                    total = taps_ref[0, :, lanes] * rows[t]
                    for u in range(t):
                        term = taps_ref[t - u, :, lanes] * rows[u]
                        if masked:
                            term = jnp.where(own[t] == own[u], term, 0.0)
                        total = total + term
                    local.append(total)
                carried = [None] * STEPS
                for mode in range(modes):
                    scan = ends_ref[inner, mode, :, lanes]
                    moved = one_ref[mode, :, lanes] * pltpu.roll(scan, 1, 0)
                    scan = scan + (moved * one_in if masked else moved)
                    moved = two_ref[mode, :, lanes] * pltpu.roll(scan, 2, 0)
                    scan = scan + (moved * two_in if masked else moved)
                    moved = four_ref[mode, :, lanes] * pltpu.roll(scan, 4, 0)
                    scan = scan + (moved * four_in if masked else moved)
                    entry = state[mode, :, lanes]
                    moved = onward_ref[mode, :, lanes] * entry
                    scan = scan + (moved * start_in if masked else moved)
                    state[mode, :, lanes] = jnp.broadcast_to(scan[SUB - 1 : SUB], (SUB, LANES))
                    running = jnp.where(rank == 0, entry, pltpu.roll(scan, 1, 0)) * scale_ref[mode, :, lanes]
                    decay = decay_ref[mode, :, lanes]
                    for t in range(STEPS):
                        running = running * decay
                        carried[t] = running if carried[t] is None else carried[t] + running
                for t in range(STEPS):
                    more = carried[t] * open_in[t] if masked else carried[t]
                    out_ref[pl.ds(inner * BLOCK + t * SUB, SUB), lanes] = local[t] + more

        @pl.when(single)
        def _():
            tiles(False)

        @pl.when(jnp.logical_not(single))
        def _():
            tiles(True)

        return unused

    lax.fori_loop(0, per, one, 0)


def mix_kernel(per, starts, first, last, arrived_ref, filtered_ref, out_ref, held):
    step = pl.program_id(0)
    place = slot_position((BLOCK, BLOCK), 1)
    row = lax.broadcasted_iota(jnp.int32, (BLOCK, BLOCK), 0)
    back = jnp.where(place == row, 1.0, 0.0).astype(BF16)

    def one(inner, unused):
        gather_block(step * per + inner, starts, first, last, arrived_ref, held)
        rows = pl.ds(inner * BLOCK, BLOCK)
        mixed = (held[...] * filtered_ref[rows, :]).astype(BF16)
        out_ref[rows, :] = jnp.dot(back, mixed, preferred_element_type=F32).astype(BF16)
        return unused

    lax.fori_loop(0, per, one, 0)


def whole(array):
    zeros = (0,) * array.ndim
    return pl.BlockSpec(array.shape, lambda i, *_: zeros)


def passed_along(value, axis, steps):
    count = lax.axis_size(axis)
    return lax.ppermute(value, axis, [(source, source + steps) for source in range(count - steps)])


def shards(streams, load_counts, seg_ids, rates, residues, skip):
    capacity = streams.shape[0]
    groups = lax.axis_size("ch")
    channels, modes = rates.shape
    length = seg_ids.shape[0]
    blocks = length // BLOCK
    per = 4
    counts = load_counts[0]
    mine = lax.axis_index("ch")
    shift = jnp.sum(jnp.where(jnp.arange(groups) < mine, counts, 0)).astype(jnp.int32)[None]
    planes = jnp.transpose(streams, (1, 0, 2))
    signal_out = send(send_signal_kernel, (1, 2), planes, shift, groups, channels, 4)
    signal_in = lax.all_to_all(signal_out, "ch", split_axis=0, concat_axis=0, tiled=True)
    query_out = send(send_query_kernel, (0,), planes, shift, groups, channels, 4)
    query_in = lax.all_to_all(query_out, "ch", split_axis=0, concat_axis=0, tiled=True)

    ending = jnp.sum(jnp.where(jnp.arange(groups)[:, None] >= jnp.arange(groups)[None, :], counts[None, :], 0), axis=1)
    starts = jnp.concatenate([jnp.zeros((1,), jnp.int32), ending]).astype(jnp.int32)
    edges = jnp.arange(blocks, dtype=jnp.int32) * BLOCK
    first = jnp.sum((ending[None, :] <= edges[:, None]).astype(jnp.int32), axis=1)
    last = jnp.sum((starts[None, :-1] < edges[:, None] + BLOCK).astype(jnp.int32), axis=1)
    bounds = jnp.sum((seg_ids[None, :] < jnp.arange(1, 4, dtype=jnp.int32)[:, None]).astype(jnp.int32), axis=1)

    rate = jnp.transpose(rates)
    gain = jnp.sqrt(-jnp.expm1(-2.0 * rate))
    scale = jnp.transpose(residues) * gain
    rank = jnp.arange(SUB, dtype=F32)[None, :, None]

    def power(exponent):
        return jnp.exp(-exponent * rate[:, None, :])

    flat = jnp.zeros((1, SUB, 1), F32)
    decay = power(1.0 + flat)
    weight = power((SUB - 1.0 - rank) * STEPS)
    leap = power(float(BLOCK) + flat)
    one_coef = jnp.where(rank >= 1, power(1.0 * STEPS + flat), 0.0)
    two_coef = jnp.where(rank >= 2, power(2.0 * STEPS + flat), 0.0)
    four_coef = jnp.where(rank >= 4, power(4.0 * STEPS + flat), 0.0)
    onward = power((rank + 1.0) * STEPS)
    scale_b = jnp.broadcast_to(scale[:, None, :], (modes, SUB, channels))
    lag = jnp.arange(STEPS, dtype=F32)[:, None, None]
    taps = jnp.sum(scale[None] * jnp.exp(-lag * rate[None]), axis=1)
    taps = taps + jnp.where(jnp.arange(STEPS)[:, None] == 0, skip[None, :], 0.0)
    taps_b = jnp.broadcast_to(taps[:, None, :], (STEPS, SUB, channels))
    span = jnp.exp(-float(length) * rate)

    coefficients = (decay, weight, leap)
    signal, ends, final = pl.pallas_call(
        functools.partial(scan_kernel, per),
        out_shape=(
            jax.ShapeDtypeStruct((length, channels), BF16),
            jax.ShapeDtypeStruct((blocks, modes, SUB, channels), F32),
            jax.ShapeDtypeStruct((modes, channels), F32),
        ),
        grid_spec=pltpu.PrefetchScalarGridSpec(
            num_scalar_prefetch=4,
            grid=(blocks // per,),
            in_specs=[whole(signal_in)] + [whole(c) for c in coefficients],
            out_specs=(
                pl.BlockSpec((per * BLOCK, channels), lambda i, *_: (i, 0)),
                pl.BlockSpec((per, modes, SUB, channels), lambda i, *_: (i, 0, 0, 0)),
                pl.BlockSpec((modes, channels), lambda i, *_: (0, 0)),
            ),
            scratch_shapes=[pltpu.VMEM((BLOCK, channels), F32), pltpu.VMEM((modes, SUB, channels), F32)],
        ),
    )(starts, first, last, bounds, signal_in, *coefficients)

    ids = jnp.stack([seg_ids[0], seg_ids[-1]]).astype(F32)
    passing = jnp.concatenate(
        [final, jnp.broadcast_to(ids[:, None], (2, channels)), jnp.zeros((SUB - 2, channels), F32)]
    )
    near = passed_along(passing, "ctx", 1)
    far = passed_along(passing, "ctx", 2)
    farther = passed_along(passing, "ctx", 3)

    resident = (near, far, farther, decay, one_coef, two_coef, four_coef, onward, scale_b, taps_b, span)
    filtered = pl.pallas_call(
        functools.partial(conv_kernel, per),
        out_shape=jax.ShapeDtypeStruct((length, channels), F32),
        grid_spec=pltpu.PrefetchScalarGridSpec(
            num_scalar_prefetch=1,
            grid=(blocks // per,),
            in_specs=[
                pl.BlockSpec((per * BLOCK, channels), lambda i, *_: (i, 0)),
                pl.BlockSpec((per, modes, SUB, channels), lambda i, *_: (i, 0, 0, 0)),
            ]
            + [whole(r) for r in resident],
            out_specs=pl.BlockSpec((per * BLOCK, channels), lambda i, *_: (i, 0)),
            scratch_shapes=[pltpu.VMEM((modes, SUB, channels), F32)],
        ),
    )(bounds, signal, ends, *resident)

    return pl.pallas_call(
        functools.partial(mix_kernel, per),
        out_shape=jax.ShapeDtypeStruct((length, channels), BF16),
        grid_spec=pltpu.PrefetchScalarGridSpec(
            num_scalar_prefetch=3,
            grid=(blocks // per,),
            in_specs=[whole(query_in), pl.BlockSpec((per * BLOCK, channels), lambda i, *_: (i, 0))],
            out_specs=pl.BlockSpec((per * BLOCK, channels), lambda i, *_: (i, 0)),
            scratch_shapes=[pltpu.VMEM((BLOCK, channels), F32)],
        ),
    )(starts, first, last, query_in, filtered)


def solution(mesh):
    return jax.shard_map(
        shards,
        mesh=mesh,
        in_specs=(
            P(("ctx", "ch"), None, None),
            P("ctx", None),
            P("ctx"),
            P("ch", None),
            P("ch", None),
            P("ch"),
        ),
        out_specs=P("ctx", "ch"),
        check_vma=False,
    )
```

```python
import functools

import jax
import jax.numpy as jnp
from jax import lax
from jax.experimental import pallas as pl
from jax.experimental.pallas import tpu as pltpu
from jax.sharding import PartitionSpec as P

BLOCK = 128
STEPS = 16
LANES = 128
SUB = 8
F32 = jnp.float32
BF16 = jnp.bfloat16


def slot_position(shape, dim):
    slot = lax.broadcasted_iota(jnp.int32, shape, dim)
    return (slot & (SUB - 1)) * STEPS + (slot >> 3)


def send_signal_kernel(key_ref, value_ref, out_ref):
    signal = key_ref[0] * value_ref[0]
    channels = out_ref.shape[2]
    for part in range(out_ref.shape[0]):
        out_ref[part] = signal[:, part * channels : (part + 1) * channels]


def send_query_kernel(shift, query_ref, out_ref):
    place = lax.broadcasted_iota(jnp.int32, (BLOCK, BLOCK), 0)
    row = lax.broadcasted_iota(jnp.int32, (BLOCK, BLOCK), 1)
    turn = jnp.where(((row + shift[0]) & (BLOCK - 1)) == place, 1.0, 0.0).astype(BF16)
    moved = jnp.dot(turn, query_ref[0], preferred_element_type=F32).astype(BF16)
    channels = out_ref.shape[2]
    for part in range(out_ref.shape[0]):
        out_ref[part] = moved[:, part * channels : (part + 1) * channels]


def send(kernel, planes, streams, scalars, groups, channels, step):
    rows = streams.shape[1]
    return pl.pallas_call(
        kernel,
        out_shape=jax.ShapeDtypeStruct((groups, rows, channels), BF16),
        grid_spec=pltpu.PrefetchScalarGridSpec(
            num_scalar_prefetch=len(scalars),
            grid=(groups // step,),
            in_specs=[
                pl.BlockSpec((1, rows, step * channels), functools.partial(lambda plane, i, *_: (plane, 0, i), plane))
                for plane in planes
            ],
            out_specs=pl.BlockSpec((step, rows, channels), lambda i, *_: (i, 0, 0)),
        ),
    )(*scalars, *[streams for _ in planes])


def segment(position, bounds):
    total = (position >= bounds[0]).astype(jnp.int32)
    for bound in bounds[1:]:
        total = total + (position >= bound).astype(jnp.int32)
    return total


def scan_kernel(starts, first, last, bounds, arrived_ref, decay_ref, weight_ref, leap_ref, signal_ref, ends_ref, final_ref, carry, gap):
    limits = [bounds[k] for k in range(3)]
    blocks, modes, _, channels = ends_ref.shape
    carry[...] = jnp.zeros_like(carry)
    row = lax.broadcasted_iota(jnp.int32, (BLOCK, BLOCK), 1)
    gap[...] = slot_position((BLOCK, BLOCK), 0) - row
    rank = lax.broadcasted_iota(jnp.int32, (SUB, LANES), 0)

    def one(block, unused):
        begin = block * BLOCK

        def picked(source):
            low = starts[source] - begin
            held = starts[source + 1] - starts[source]
            here = (gap[...] == low) & (row < held)
            return jnp.dot(
                jnp.where(here, 1.0, 0.0).astype(BF16), arrived_ref[source], preferred_element_type=F32
            )

        rows_here = pl.ds(pl.multiple_of(begin, BLOCK), BLOCK)
        signal_ref[rows_here, :] = picked(first[block])

        def add(source, carried):
            signal_ref[rows_here, :] += picked(source)
            return carried

        lax.fori_loop(first[block] + 1, last[block], add, 0)
        first_id = segment(begin, limits)
        last_id = segment(begin + BLOCK - 1, limits)
        before_id = segment(begin - 1, limits)
        reach = segment(begin + rank * STEPS + STEPS - 1, limits) == last_id
        going = jnp.where(before_id == last_id, 1.0, 0.0)

        def tiles(masked):
            if masked:
                own = [segment(begin + rank * STEPS + t, limits) for t in range(STEPS)]
            for tile in range(channels // LANES):
                lanes = pl.ds(tile * LANES, LANES)
                rows = [
                    signal_ref[pl.ds(pl.multiple_of(begin + t * SUB, SUB), SUB), lanes] for t in range(STEPS)
                ]
                if masked:
                    rows = [jnp.where(o == own[-1], r, 0.0) for o, r in zip(own, rows)]
                for mode in range(modes):
                    decay = decay_ref[mode, :, lanes]
                    state = rows[0]
                    for t in range(1, STEPS):
                        state = decay * state + rows[t]
                    ends_ref[block, mode, :, lanes] = state
                    kept = weight_ref[mode, :, lanes] * state
                    if masked:
                        kept = jnp.where(reach, kept, 0.0)
                    carry[mode, :, lanes] = (going * leap_ref[mode, :, lanes]) * carry[mode, :, lanes] + kept

        @pl.when(first_id == last_id)
        def _():
            tiles(False)

        @pl.when(first_id != last_id)
        def _():
            tiles(True)

        return unused

    lax.fori_loop(0, blocks, one, 0)
    final_ref[...] = jnp.sum(carry[...], axis=1)


def conv_kernel(
    bounds, signal_ref, ends_ref, near_ref, far_ref, farther_ref, decay_ref, one_ref, two_ref, four_ref, onward_ref, scale_ref, taps_ref, span_ref, out_ref, state
):
    limits = [bounds[k] for k in range(3)]
    blocks, modes, _, channels = ends_ref.shape
    start_id = segment(0, limits).astype(F32)

    def ids(ref):
        return ref[modes : modes + 1, :], ref[modes + 1 : modes + 2, :]

    near_first, near_last = ids(near_ref)
    far_first, far_last = ids(far_ref)
    _, farther_last = ids(farther_ref)
    through_far = jnp.where((far_first == far_last) & (far_first == farther_last), 1.0, 0.0)
    through_near = jnp.where((near_first == near_last) & (near_first == far_last), 1.0, 0.0)
    entering = jnp.where(near_last == start_id, 1.0, 0.0)
    span = span_ref[...]
    inside = far_ref[0:modes, :] + through_far * span * farther_ref[0:modes, :]
    inside = near_ref[0:modes, :] + through_near * span * inside
    inside = entering * inside
    for mode in range(modes):
        state[mode] = jnp.broadcast_to(inside[mode : mode + 1], (SUB, channels))

    rank = lax.broadcasted_iota(jnp.int32, (SUB, LANES), 0)

    def one(block, unused):
        begin = block * BLOCK
        last_id = segment(begin + BLOCK - 1, limits)
        before_id = segment(jnp.maximum(begin - 1, 0), limits)
        edge = segment(begin + rank * STEPS + STEPS - 1, limits)
        single = before_id == last_id

        def tiles(masked):
            if masked:
                one_in = jnp.where((rank >= 1) & (edge == pltpu.roll(edge, 1, 0)), 1.0, 0.0)
                two_in = jnp.where((rank >= 2) & (edge == pltpu.roll(edge, 2, 0)), 1.0, 0.0)
                four_in = jnp.where((rank >= 4) & (edge == pltpu.roll(edge, 4, 0)), 1.0, 0.0)
                start_in = jnp.where(edge == before_id, 1.0, 0.0)
                prior = jnp.where(rank == 0, before_id, pltpu.roll(edge, 1, 0))
                own = [segment(begin + rank * STEPS + t, limits) for t in range(STEPS)]
                open_in = [jnp.where(o == prior, 1.0, 0.0) for o in own]
            for tile in range(channels // LANES):
                lanes = pl.ds(tile * LANES, LANES)
                rows = [
                    signal_ref[pl.ds(pl.multiple_of(begin + t * SUB, SUB), SUB), lanes] for t in range(STEPS)
                ]
                local = []
                for t in range(STEPS):
                    total = taps_ref[0, :, lanes] * rows[t]
                    for u in range(t):
                        term = taps_ref[t - u, :, lanes] * rows[u]
                        if masked:
                            term = jnp.where(own[t] == own[u], term, 0.0)
                        total = total + term
                    local.append(total)
                carried = [None] * STEPS
                for mode in range(modes):
                    scan = ends_ref[block, mode, :, lanes]
                    moved = one_ref[mode, :, lanes] * pltpu.roll(scan, 1, 0)
                    scan = scan + (moved * one_in if masked else moved)
                    moved = two_ref[mode, :, lanes] * pltpu.roll(scan, 2, 0)
                    scan = scan + (moved * two_in if masked else moved)
                    moved = four_ref[mode, :, lanes] * pltpu.roll(scan, 4, 0)
                    scan = scan + (moved * four_in if masked else moved)
                    entry = state[mode, :, lanes]
                    moved = onward_ref[mode, :, lanes] * entry
                    scan = scan + (moved * start_in if masked else moved)
                    state[mode, :, lanes] = jnp.broadcast_to(scan[SUB - 1 : SUB], (SUB, LANES))
                    running = jnp.where(rank == 0, entry, pltpu.roll(scan, 1, 0)) * scale_ref[mode, :, lanes]
                    decay = decay_ref[mode, :, lanes]
                    for t in range(STEPS):
                        running = running * decay
                        carried[t] = running if carried[t] is None else carried[t] + running
                for t in range(STEPS):
                    more = carried[t] * open_in[t] if masked else carried[t]
                    out_ref[tile, pl.ds(begin + t, SUB, stride=STEPS), :] = local[t] + more

        @pl.when(single)
        def _():
            tiles(False)

        @pl.when(jnp.logical_not(single))
        def _():
            tiles(True)

        return unused

    lax.fori_loop(0, blocks, one, 0)


def mix_kernel(starts, first, last, arrived_ref, filtered_ref, out_ref, held, ready, sems):
    pieces = sems.shape[0]
    blocks = filtered_ref.shape[1] // BLOCK
    per = blocks // pieces
    place = lax.broadcasted_iota(jnp.int32, (BLOCK, LANES), 0)
    tiles = held.shape[1] // LANES

    def one(block, unused):
        begin = pl.multiple_of(block * BLOCK, BLOCK)

        def add(source, carried):
            low = starts[source] - begin
            here = place >= low
            for tile in range(tiles):
                lanes = pl.ds(tile * LANES, LANES)
                held[:, lanes] = jnp.where(here, arrived_ref[source, :, lanes].astype(F32), held[:, lanes])
            return carried

        lax.fori_loop(first[block], last[block], add, 0)
        rows = pl.ds(begin, BLOCK)
        for tile in range(tiles):
            lanes = pl.ds(tile * LANES, LANES)
            ready[rows, lanes] = (held[:, lanes] * filtered_ref[tile, rows, :]).astype(BF16)
        return unused

    def copy(piece):
        rows = pl.ds(piece * per * BLOCK, per * BLOCK)
        return pltpu.make_async_copy(ready.at[rows, :], out_ref.at[rows, :], sems.at[piece])

    for piece in range(pieces):
        lax.fori_loop(piece * per, (piece + 1) * per, one, 0)
        copy(piece).start()
    for piece in range(pieces):
        copy(piece).wait()


def near_by(array):
    return pltpu.with_memory_space_constraint(array, pltpu.VMEM)


def local_call(kernel, outs, scalars, arrays, scratch, out_space=pltpu.VMEM):
    return pl.pallas_call(
        kernel,
        out_shape=outs,
        in_specs=[pl.BlockSpec(memory_space=pltpu.SMEM)] * len(scalars) + [pl.BlockSpec(memory_space=pltpu.VMEM)] * len(arrays),
        out_specs=jax.tree.map(lambda _: pl.BlockSpec(memory_space=out_space), outs),
        scratch_shapes=scratch,
        compiler_params=pltpu.CompilerParams(vmem_limit_bytes=24 << 20),
    )(*scalars, *[near_by(array) for array in arrays])


def passed_along(value, axis, steps):
    count = lax.axis_size(axis)
    return lax.ppermute(value, axis, [(source, source + steps) for source in range(count - steps)])


def shards(streams, load_counts, seg_ids, rates, residues, skip):
    capacity = streams.shape[0]
    groups = lax.axis_size("ch")
    channels, modes = rates.shape
    length = seg_ids.shape[0]
    blocks = length // BLOCK
    counts = load_counts[0]
    planes = jnp.transpose(streams, (1, 0, 2))
    signal_out = send(send_signal_kernel, (1, 2), planes, (), groups, channels, 8)
    signal_in = lax.all_to_all(signal_out, "ch", split_axis=0, concat_axis=0, tiled=True)
    mine = lax.axis_index("ch")
    shift = jnp.sum(jnp.where(jnp.arange(groups) < mine, counts, 0)).astype(jnp.int32)[None]
    query_out = send(send_query_kernel, (0,), planes, (shift,), groups, channels, 8)

    ending = jnp.sum(jnp.where(jnp.arange(groups)[:, None] >= jnp.arange(groups)[None, :], counts[None, :], 0), axis=1)
    starts = jnp.concatenate([jnp.zeros((1,), jnp.int32), ending]).astype(jnp.int32)
    edges = jnp.arange(blocks, dtype=jnp.int32) * BLOCK
    first = jnp.sum((ending[None, :] <= edges[:, None]).astype(jnp.int32), axis=1)
    last = jnp.sum((starts[None, :-1] < edges[:, None] + BLOCK).astype(jnp.int32), axis=1)
    bounds = jnp.sum((seg_ids[None, :] < jnp.arange(1, 4, dtype=jnp.int32)[:, None]).astype(jnp.int32), axis=1)

    rate = jnp.transpose(rates)
    gain = jnp.sqrt(-jnp.expm1(-2.0 * rate))
    scale = jnp.transpose(residues) * gain
    rank = jnp.arange(SUB, dtype=F32)[None, :, None]

    def power(exponent):
        return jnp.exp(-exponent * rate[:, None, :])

    flat = jnp.zeros((1, SUB, 1), F32)
    decay = power(1.0 + flat)
    weight = power((SUB - 1.0 - rank) * STEPS)
    leap = power(float(BLOCK) + flat)
    one_coef = jnp.where(rank >= 1, power(1.0 * STEPS + flat), 0.0)
    two_coef = jnp.where(rank >= 2, power(2.0 * STEPS + flat), 0.0)
    four_coef = jnp.where(rank >= 4, power(4.0 * STEPS + flat), 0.0)
    onward = power((rank + 1.0) * STEPS)
    scale_b = jnp.broadcast_to(scale[:, None, :], (modes, SUB, channels))
    lag = jnp.arange(STEPS, dtype=F32)[:, None, None]
    taps = jnp.sum(scale[None] * jnp.exp(-lag * rate[None]), axis=1)
    taps = taps + jnp.where(jnp.arange(STEPS)[:, None] == 0, skip[None, :], 0.0)
    taps_b = jnp.broadcast_to(taps[:, None, :], (STEPS, SUB, channels))
    span = jnp.exp(-float(length) * rate)

    prepared = (starts, first, last, bounds, decay, weight, leap, one_coef, two_coef, four_coef, onward, scale_b, taps_b, span)
    query_out, prepared = lax.optimization_barrier((query_out, prepared))
    starts, first, last, bounds, decay, weight, leap, one_coef, two_coef, four_coef, onward, scale_b, taps_b, span = prepared
    query_in = lax.all_to_all(query_out, "ch", split_axis=0, concat_axis=0, tiled=True)

    signal, ends, final = local_call(
        scan_kernel,
        (
            pltpu.VMEM((length, channels), F32),
            pltpu.VMEM((blocks, modes, SUB, channels), F32),
            pltpu.VMEM((modes, channels), F32),
        ),
        (starts, first, last, bounds),
        (signal_in, decay, weight, leap),
        [pltpu.VMEM((modes, SUB, channels), F32), pltpu.VMEM((BLOCK, BLOCK), jnp.int32)],
    )

    ids = jnp.stack([seg_ids[0], seg_ids[-1]]).astype(F32)
    passing = jnp.concatenate(
        [final, jnp.broadcast_to(ids[:, None], (2, channels)), jnp.zeros((SUB - 2, channels), F32)]
    )
    near = passed_along(passing, "ctx", 1)
    far = passed_along(passing, "ctx", 2)
    farther = passed_along(passing, "ctx", 3)

    filtered = local_call(
        conv_kernel,
        pltpu.VMEM((channels // LANES, length, LANES), F32),
        (bounds,),
        (signal, ends, near, far, farther, decay, one_coef, two_coef, four_coef, onward, scale_b, taps_b, span),
        [pltpu.VMEM((modes, SUB, channels), F32)],
    )
    pieces = 4
    return local_call(
        mix_kernel,
        jax.ShapeDtypeStruct((length, channels), BF16),
        (starts, first, last),
        (query_in, filtered),
        [
            pltpu.VMEM((BLOCK, channels), F32),
            pltpu.VMEM((length, channels), BF16),
            pltpu.SemaphoreType.DMA((pieces,)),
        ],
        pl.ANY,
    )


def solution(mesh):
    return jax.shard_map(
        shards,
        mesh=mesh,
        in_specs=(
            P(("ctx", "ch"), None, None),
            P("ctx", None),
            P("ctx"),
            P("ch", None),
            P("ch", None),
            P("ch"),
        ),
        out_specs=P("ctx", "ch"),
        check_vma=False,
    )
```

```python
import functools

import jax
import jax.numpy as jnp
from jax import lax
from jax.experimental import pallas as pl
from jax.experimental.pallas import tpu as pltpu
from jax.sharding import PartitionSpec as P

BLOCK = 128
STEPS = 16
LANES = 128
SUB = 8
F32 = jnp.float32
BF16 = jnp.bfloat16


def send_signal_kernel(key_ref, value_ref, out_ref):
    signal = key_ref[0] * value_ref[0]
    channels = out_ref.shape[2]
    for part in range(out_ref.shape[0]):
        out_ref[part] = signal[:, part * channels : (part + 1) * channels]


def send_query_kernel(query_ref, out_ref):
    channels = out_ref.shape[2]
    for part in range(out_ref.shape[0]):
        out_ref[part] = query_ref[0, :, part * channels : (part + 1) * channels]


def send(kernel, planes, streams, groups, channels, step):
    rows = streams.shape[1]
    return pl.pallas_call(
        kernel,
        out_shape=jax.ShapeDtypeStruct((groups, rows, channels), BF16),
        grid=(groups // step,),
        in_specs=[
            pl.BlockSpec((1, rows, step * channels), functools.partial(lambda plane, i: (plane, 0, i), plane))
            for plane in planes
        ],
        out_specs=pl.BlockSpec((step, rows, channels), lambda i: (i, 0, 0)),
    )(*[streams for _ in planes])


def compact(starts, arrived_ref, into_ref):
    sources, rows, channels = arrived_ref.shape

    def place(source, unused):
        begin = starts[source]
        for part in range(0, rows, 2 * SUB):
            for tile in range(channels // LANES):
                piece = arrived_ref[source, pl.ds(part, 2 * SUB), pl.ds(tile * LANES, LANES)].astype(F32)
                into_ref[tile, pl.ds(begin + part, SUB), :] = piece[:SUB]
                into_ref[tile, pl.ds(begin + part + SUB, SUB), :] = piece[SUB:]
        return unused

    lax.fori_loop(0, sources, place, 0)


def segment(position, bounds):
    total = (position >= bounds[0]).astype(jnp.int32)
    for bound in bounds[1:]:
        total = total + (position >= bound).astype(jnp.int32)
    return total


def scan_kernel(starts, bounds, arrived_ref, decay_ref, weight_ref, leap_ref, signal_ref, ends_ref, passing_ref, carry):
    limits = [bounds[k] for k in range(3)]
    blocks, modes, _, channels = ends_ref.shape
    carry[...] = jnp.zeros_like(carry)
    rank = lax.broadcasted_iota(jnp.int32, (SUB, LANES), 0)
    compact(starts, arrived_ref, signal_ref)

    def one(block, unused):
        begin = block * BLOCK
        first_id = segment(begin, limits)
        last_id = segment(begin + BLOCK - 1, limits)
        before_id = segment(begin - 1, limits)
        reach = segment(begin + rank * STEPS + STEPS - 1, limits) == last_id
        going = jnp.where(before_id == last_id, 1.0, 0.0)

        def tiles(masked):
            if masked:
                own = [segment(begin + rank * STEPS + t, limits) for t in range(STEPS)]
            for tile in range(channels // LANES):
                lanes = pl.ds(tile * LANES, LANES)
                rows = [signal_ref[tile, pl.ds(begin + t, SUB, stride=STEPS), :] for t in range(STEPS)]
                if masked:
                    rows = [jnp.where(o == own[-1], r, 0.0) for o, r in zip(own, rows)]
                for mode in range(modes):
                    decay = decay_ref[mode, :, lanes]
                    state = rows[0]
                    for t in range(1, STEPS):
                        state = decay * state + rows[t]
                    ends_ref[block, mode, :, lanes] = state
                    kept = weight_ref[mode, :, lanes] * state
                    if masked:
                        kept = jnp.where(reach, kept, 0.0)
                    carry[mode, :, lanes] = (going * leap_ref[mode, :, lanes]) * carry[mode, :, lanes] + kept

        @pl.when(first_id == last_id)
        def _():
            tiles(False)

        @pl.when(first_id != last_id)
        def _():
            tiles(True)

        return unused

    lax.fori_loop(0, blocks, one, 0)
    passing_ref[0:modes, :] = jnp.sum(carry[...], axis=1)
    line = lax.broadcasted_iota(jnp.int32, (SUB, channels), 0)
    ids = jnp.where(line == 0, segment(0, limits), segment(blocks * BLOCK - 1, limits))
    passing_ref[modes : modes + SUB, :] = ids.astype(F32)


def conv_kernel(
    bounds, signal_ref, ends_ref, near_ref, far_ref, farther_ref, decay_ref, one_ref, two_ref, four_ref, onward_ref, scale_ref, taps_ref, span_ref, out_ref, state
):
    limits = [bounds[k] for k in range(3)]
    blocks, modes, _, channels = ends_ref.shape
    start_id = segment(0, limits).astype(F32)

    def ids(ref):
        return ref[modes : modes + 1, :], ref[modes + 1 : modes + 2, :]

    near_first, near_last = ids(near_ref)
    far_first, far_last = ids(far_ref)
    _, farther_last = ids(farther_ref)
    through_far = jnp.where((far_first == far_last) & (far_first == farther_last), 1.0, 0.0)
    through_near = jnp.where((near_first == near_last) & (near_first == far_last), 1.0, 0.0)
    entering = jnp.where(near_last == start_id, 1.0, 0.0)
    span = span_ref[...]
    inside = far_ref[0:modes, :] + through_far * span * farther_ref[0:modes, :]
    inside = near_ref[0:modes, :] + through_near * span * inside
    inside = entering * inside
    for mode in range(modes):
        state[mode] = jnp.broadcast_to(inside[mode : mode + 1], (SUB, channels))

    rank = lax.broadcasted_iota(jnp.int32, (SUB, LANES), 0)

    def one(block, unused):
        begin = block * BLOCK
        last_id = segment(begin + BLOCK - 1, limits)
        before_id = segment(jnp.maximum(begin - 1, 0), limits)
        edge = segment(begin + rank * STEPS + STEPS - 1, limits)
        single = before_id == last_id

        def tiles(masked):
            if masked:
                one_in = jnp.where((rank >= 1) & (edge == pltpu.roll(edge, 1, 0)), 1.0, 0.0)
                two_in = jnp.where((rank >= 2) & (edge == pltpu.roll(edge, 2, 0)), 1.0, 0.0)
                four_in = jnp.where((rank >= 4) & (edge == pltpu.roll(edge, 4, 0)), 1.0, 0.0)
                start_in = jnp.where(edge == before_id, 1.0, 0.0)
                prior = jnp.where(rank == 0, before_id, pltpu.roll(edge, 1, 0))
                own = [segment(begin + rank * STEPS + t, limits) for t in range(STEPS)]
                open_in = [jnp.where(o == prior, 1.0, 0.0) for o in own]
            for tile in range(channels // LANES):
                lanes = pl.ds(tile * LANES, LANES)
                rows = [signal_ref[tile, pl.ds(begin + t, SUB, stride=STEPS), :] for t in range(STEPS)]
                local = []
                for t in range(STEPS):
                    total = taps_ref[0, :, lanes] * rows[t]
                    for u in range(t):
                        term = taps_ref[t - u, :, lanes] * rows[u]
                        if masked:
                            term = jnp.where(own[t] == own[u], term, 0.0)
                        total = total + term
                    local.append(total)
                carried = [None] * STEPS
                for mode in range(modes):
                    scan = ends_ref[block, mode, :, lanes]
                    moved = one_ref[mode, :, lanes] * pltpu.roll(scan, 1, 0)
                    scan = scan + (moved * one_in if masked else moved)
                    moved = two_ref[mode, :, lanes] * pltpu.roll(scan, 2, 0)
                    scan = scan + (moved * two_in if masked else moved)
                    moved = four_ref[mode, :, lanes] * pltpu.roll(scan, 4, 0)
                    scan = scan + (moved * four_in if masked else moved)
                    entry = state[mode, :, lanes]
                    moved = onward_ref[mode, :, lanes] * entry
                    scan = scan + (moved * start_in if masked else moved)
                    state[mode, :, lanes] = jnp.broadcast_to(scan[SUB - 1 : SUB], (SUB, LANES))
                    running = jnp.where(rank == 0, entry, pltpu.roll(scan, 1, 0)) * scale_ref[mode, :, lanes]
                    decay = decay_ref[mode, :, lanes]
                    for t in range(STEPS):
                        running = running * decay
                        carried[t] = running if carried[t] is None else carried[t] + running
                for t in range(STEPS):
                    more = carried[t] * open_in[t] if masked else carried[t]
                    out_ref[tile, pl.ds(begin + t, SUB, stride=STEPS), :] = local[t] + more

        @pl.when(single)
        def _():
            tiles(False)

        @pl.when(jnp.logical_not(single))
        def _():
            tiles(True)

        return unused

    lax.fori_loop(0, blocks, one, 0)


def mix_kernel(starts, arrived_ref, filtered_ref, out_ref, held, ready, sems):
    pieces = sems.shape[0]
    tiles, length, _ = filtered_ref.shape
    per = length // BLOCK // pieces
    compact(starts, arrived_ref, held)

    def one(block, unused):
        rows = pl.ds(pl.multiple_of(block * BLOCK, BLOCK), BLOCK)
        for tile in range(tiles):
            ready[rows, pl.ds(tile * LANES, LANES)] = (held[tile, rows, :] * filtered_ref[tile, rows, :]).astype(BF16)
        return unused

    def copy(piece):
        rows = pl.ds(piece * per * BLOCK, per * BLOCK)
        return pltpu.make_async_copy(ready.at[rows, :], out_ref.at[rows, :], sems.at[piece])

    for piece in range(pieces):
        lax.fori_loop(piece * per, (piece + 1) * per, one, 0)
        copy(piece).start()
    for piece in range(pieces):
        copy(piece).wait()


def near_by(array):
    return pltpu.with_memory_space_constraint(array, pltpu.VMEM)


def local_call(kernel, outs, scalars, arrays, scratch, out_space=pltpu.VMEM):
    return pl.pallas_call(
        kernel,
        out_shape=outs,
        in_specs=[pl.BlockSpec(memory_space=pltpu.SMEM)] * len(scalars) + [pl.BlockSpec(memory_space=pltpu.VMEM)] * len(arrays),
        out_specs=jax.tree.map(lambda _: pl.BlockSpec(memory_space=out_space), outs),
        scratch_shapes=scratch,
        compiler_params=pltpu.CompilerParams(vmem_limit_bytes=24 << 20),
    )(*scalars, *[near_by(array) for array in arrays])


def passed_along(value, axis, steps):
    count = lax.axis_size(axis)
    return lax.ppermute(value, axis, [(source, source + steps) for source in range(count - steps)])


def shards(streams, load_counts, seg_ids, rates, residues, skip):
    capacity = streams.shape[0]
    groups = lax.axis_size("ch")
    channels, modes = rates.shape
    length = seg_ids.shape[0]
    blocks = length // BLOCK
    counts = load_counts[0]
    planes = jnp.transpose(streams, (1, 0, 2))
    signal_out = send(send_signal_kernel, (1, 2), planes, groups, channels, 8)
    signal_in = lax.all_to_all(signal_out, "ch", split_axis=0, concat_axis=0, tiled=True)
    query_out = send(send_query_kernel, (0,), planes, groups, channels, 8)

    ending = jnp.sum(jnp.where(jnp.arange(groups)[:, None] >= jnp.arange(groups)[None, :], counts[None, :], 0), axis=1)
    starts = jnp.concatenate([jnp.zeros((1,), jnp.int32), ending]).astype(jnp.int32)
    bounds = jnp.sum((seg_ids[None, :] < jnp.arange(1, 4, dtype=jnp.int32)[:, None]).astype(jnp.int32), axis=1)

    rate = jnp.transpose(rates)
    gain = jnp.sqrt(-jnp.expm1(-2.0 * rate))
    scale = jnp.transpose(residues) * gain
    rank = jnp.arange(SUB, dtype=F32)[None, :, None]

    def power(exponent):
        return jnp.exp(-exponent * rate[:, None, :])

    flat = jnp.zeros((1, SUB, 1), F32)
    decay = power(1.0 + flat)
    weight = power((SUB - 1.0 - rank) * STEPS)
    leap = power(float(BLOCK) + flat)
    one_coef = jnp.where(rank >= 1, power(1.0 * STEPS + flat), 0.0)
    two_coef = jnp.where(rank >= 2, power(2.0 * STEPS + flat), 0.0)
    four_coef = jnp.where(rank >= 4, power(4.0 * STEPS + flat), 0.0)
    onward = power((rank + 1.0) * STEPS)
    scale_b = jnp.broadcast_to(scale[:, None, :], (modes, SUB, channels))
    lag = jnp.arange(STEPS, dtype=F32)[:, None, None]
    taps = jnp.sum(scale[None] * jnp.exp(-lag * rate[None]), axis=1)
    taps = taps + jnp.where(jnp.arange(STEPS)[:, None] == 0, skip[None, :], 0.0)
    taps_b = jnp.broadcast_to(taps[:, None, :], (STEPS, SUB, channels))
    span = jnp.exp(-float(length) * rate)

    prepared = (starts, bounds, decay, weight, leap, one_coef, two_coef, four_coef, onward, scale_b, taps_b, span)
    query_out, prepared = lax.optimization_barrier((query_out, prepared))
    starts, bounds, decay, weight, leap, one_coef, two_coef, four_coef, onward, scale_b, taps_b, span = prepared
    query_in = lax.all_to_all(query_out, "ch", split_axis=0, concat_axis=0, tiled=True)

    padded = (channels // LANES, length + capacity, LANES)
    signal, ends, passing = local_call(
        scan_kernel,
        (
            pltpu.VMEM(padded, F32),
            pltpu.VMEM((blocks, modes, SUB, channels), F32),
            pltpu.VMEM((modes + SUB, channels), F32),
        ),
        (starts, bounds),
        (signal_in, decay, weight, leap),
        [pltpu.VMEM((modes, SUB, channels), F32)],
    )
    near = passed_along(passing, "ctx", 1)
    far = passed_along(passing, "ctx", 2)
    farther = passed_along(passing, "ctx", 3)

    filtered = local_call(
        conv_kernel,
        pltpu.VMEM((channels // LANES, length, LANES), F32),
        (bounds,),
        (signal, ends, near, far, farther, decay, one_coef, two_coef, four_coef, onward, scale_b, taps_b, span),
        [pltpu.VMEM((modes, SUB, channels), F32)],
    )
    pieces = 4
    return local_call(
        mix_kernel,
        jax.ShapeDtypeStruct((length, channels), BF16),
        (starts,),
        (query_in, filtered),
        [
            pltpu.VMEM(padded, F32),
            pltpu.VMEM((length, channels), BF16),
            pltpu.SemaphoreType.DMA((pieces,)),
        ],
        pl.ANY,
    )


def solution(mesh):
    return jax.shard_map(
        shards,
        mesh=mesh,
        in_specs=(
            P(("ctx", "ch"), None, None),
            P("ctx", None),
            P("ctx"),
            P("ch", None),
            P("ch", None),
            P("ch"),
        ),
        out_specs=P("ctx", "ch"),
        check_vma=False,
    )
```

```python
import functools

import jax
import jax.numpy as jnp
from jax import lax
from jax.experimental import pallas as pl
from jax.experimental.pallas import tpu as pltpu
from jax.sharding import PartitionSpec as P

BLOCK = 128
STEPS = 16
LANES = 128
SUB = 8
TURN = 12
F32 = jnp.float32
BF16 = jnp.bfloat16


def send_kernel(planes, turn, streams_ref, out_ref, *scratch):
    held, ready, in_sems, out_sems = scratch[:-3], scratch[-3], scratch[-2], scratch[-1]
    pieces = in_sems.shape[1]
    groups, _, channels = out_ref.shape
    per = groups // pieces
    width = per * channels

    def load(plane, piece):
        columns = pl.ds(piece * width, width)
        return pltpu.make_async_copy(
            streams_ref.at[planes[plane], :, columns], held[plane].at[:, columns], in_sems.at[plane, piece]
        )

    def store(piece):
        goes = (piece * per + turn) % groups
        return pltpu.make_async_copy(ready.at[pl.ds(piece * per, per)], out_ref.at[pl.ds(goes, per)], out_sems.at[piece])

    for piece in range(pieces):
        for plane in range(len(planes)):
            load(plane, piece).start()
    for piece in range(pieces):
        for plane in range(len(planes)):
            load(plane, piece).wait()
        for part in range(piece * per, (piece + 1) * per):
            columns = pl.ds(part * channels, channels)
            value = held[0][:, columns]
            for other in held[1:]:
                value = value * other[:, columns]
            ready[part] = value
        store(piece).start()
    for piece in range(pieces):
        store(piece).wait()


def send(planes, streams, groups, channels, turn, pieces):
    rows = streams.shape[1]
    return pl.pallas_call(
        functools.partial(send_kernel, planes, turn),
        out_shape=jax.ShapeDtypeStruct((groups, rows, channels), BF16),
        in_specs=[pl.BlockSpec(memory_space=pl.ANY)],
        out_specs=pl.BlockSpec(memory_space=pl.ANY),
        scratch_shapes=[pltpu.VMEM((rows, groups * channels), BF16) for _ in planes]
        + [
            pltpu.VMEM((groups, rows, channels), BF16),
            pltpu.SemaphoreType.DMA((len(planes), pieces)),
            pltpu.SemaphoreType.DMA((pieces,)),
        ],
        compiler_params=pltpu.CompilerParams(vmem_limit_bytes=24 << 20),
    )(streams)


def exchange(value, order):
    return lax.all_to_all(value, "ch", split_axis=0, concat_axis=0, axis_index_groups=[order], tiled=True)


def compact(turn, starts, arrived_ref, into_ref):
    sources, rows, channels = arrived_ref.shape

    def place(source, unused):
        begin = starts[source]
        slot = lax.rem(source + turn, sources)
        for part in range(0, rows, 2 * SUB):
            for tile in range(channels // LANES):
                piece = arrived_ref[slot, pl.ds(part, 2 * SUB), pl.ds(tile * LANES, LANES)].astype(F32)
                into_ref[tile, pl.ds(begin + part, SUB), :] = piece[:SUB]
                into_ref[tile, pl.ds(begin + part + SUB, SUB), :] = piece[SUB:]
        return unused

    lax.fori_loop(0, sources, place, 0)


def segment(position, bounds):
    total = (position >= bounds[0]).astype(jnp.int32)
    for bound in bounds[1:]:
        total = total + (position >= bound).astype(jnp.int32)
    return total


def scan_kernel(turn, starts, bounds, arrived_ref, decay_ref, weight_ref, leap_ref, signal_ref, ends_ref, passing_ref, carry):
    limits = [bounds[k] for k in range(3)]
    blocks, modes, _, channels = ends_ref.shape
    carry[...] = jnp.zeros_like(carry)
    rank = lax.broadcasted_iota(jnp.int32, (SUB, LANES), 0)
    compact(turn, starts, arrived_ref, signal_ref)

    def one(block, unused):
        begin = block * BLOCK
        first_id = segment(begin, limits)
        last_id = segment(begin + BLOCK - 1, limits)
        before_id = segment(begin - 1, limits)
        reach = segment(begin + rank * STEPS + STEPS - 1, limits) == last_id
        going = jnp.where(before_id == last_id, 1.0, 0.0)

        def tiles(masked):
            if masked:
                own = [segment(begin + rank * STEPS + t, limits) for t in range(STEPS)]
            for tile in range(channels // LANES):
                lanes = pl.ds(tile * LANES, LANES)
                rows = [signal_ref[tile, pl.ds(begin + t, SUB, stride=STEPS), :] for t in range(STEPS)]
                if masked:
                    rows = [jnp.where(o == own[-1], r, 0.0) for o, r in zip(own, rows)]
                for mode in range(modes):
                    decay = decay_ref[mode, :, lanes]
                    state = rows[0]
                    for t in range(1, STEPS):
                        state = decay * state + rows[t]
                    ends_ref[block, mode, :, lanes] = state
                    kept = weight_ref[mode, :, lanes] * state
                    if masked:
                        kept = jnp.where(reach, kept, 0.0)
                    carry[mode, :, lanes] = (going * leap_ref[mode, :, lanes]) * carry[mode, :, lanes] + kept

        @pl.when(first_id == last_id)
        def _():
            tiles(False)

        @pl.when(first_id != last_id)
        def _():
            tiles(True)

        return unused

    lax.fori_loop(0, blocks, one, 0)
    passing_ref[0:modes, :] = jnp.sum(carry[...], axis=1)
    line = lax.broadcasted_iota(jnp.int32, (SUB, channels), 0)
    ids = jnp.where(line == 0, segment(0, limits), segment(blocks * BLOCK - 1, limits))
    passing_ref[modes : modes + SUB, :] = ids.astype(F32)


def conv_kernel(
    bounds, signal_ref, ends_ref, near_ref, far_ref, farther_ref, decay_ref, one_ref, two_ref, four_ref, onward_ref, scale_ref, taps_ref, span_ref, out_ref, state
):
    limits = [bounds[k] for k in range(3)]
    blocks, modes, _, channels = ends_ref.shape
    start_id = segment(0, limits).astype(F32)

    def ids(ref):
        return ref[modes : modes + 1, :], ref[modes + 1 : modes + 2, :]

    near_first, near_last = ids(near_ref)
    far_first, far_last = ids(far_ref)
    _, farther_last = ids(farther_ref)
    through_far = jnp.where((far_first == far_last) & (far_first == farther_last), 1.0, 0.0)
    through_near = jnp.where((near_first == near_last) & (near_first == far_last), 1.0, 0.0)
    entering = jnp.where(near_last == start_id, 1.0, 0.0)
    span = span_ref[...]
    inside = far_ref[0:modes, :] + through_far * span * farther_ref[0:modes, :]
    inside = near_ref[0:modes, :] + through_near * span * inside
    inside = entering * inside
    for mode in range(modes):
        state[mode] = jnp.broadcast_to(inside[mode : mode + 1], (SUB, channels))

    rank = lax.broadcasted_iota(jnp.int32, (SUB, LANES), 0)

    def one(block, unused):
        begin = block * BLOCK
        last_id = segment(begin + BLOCK - 1, limits)
        before_id = segment(jnp.maximum(begin - 1, 0), limits)
        edge = segment(begin + rank * STEPS + STEPS - 1, limits)
        single = before_id == last_id

        def tiles(masked):
            if masked:
                one_in = jnp.where((rank >= 1) & (edge == pltpu.roll(edge, 1, 0)), 1.0, 0.0)
                two_in = jnp.where((rank >= 2) & (edge == pltpu.roll(edge, 2, 0)), 1.0, 0.0)
                four_in = jnp.where((rank >= 4) & (edge == pltpu.roll(edge, 4, 0)), 1.0, 0.0)
                start_in = jnp.where(edge == before_id, 1.0, 0.0)
                prior = jnp.where(rank == 0, before_id, pltpu.roll(edge, 1, 0))
                own = [segment(begin + rank * STEPS + t, limits) for t in range(STEPS)]
                open_in = [jnp.where(o == prior, 1.0, 0.0) for o in own]
            for tile in range(channels // LANES):
                lanes = pl.ds(tile * LANES, LANES)
                rows = [signal_ref[tile, pl.ds(begin + t, SUB, stride=STEPS), :] for t in range(STEPS)]
                local = []
                for t in range(STEPS):
                    total = taps_ref[0, :, lanes] * rows[t]
                    for u in range(t):
                        term = taps_ref[t - u, :, lanes] * rows[u]
                        if masked:
                            term = jnp.where(own[t] == own[u], term, 0.0)
                        total = total + term
                    local.append(total)
                carried = [None] * STEPS
                for mode in range(modes):
                    scan = ends_ref[block, mode, :, lanes]
                    moved = one_ref[mode, :, lanes] * pltpu.roll(scan, 1, 0)
                    scan = scan + (moved * one_in if masked else moved)
                    moved = two_ref[mode, :, lanes] * pltpu.roll(scan, 2, 0)
                    scan = scan + (moved * two_in if masked else moved)
                    moved = four_ref[mode, :, lanes] * pltpu.roll(scan, 4, 0)
                    scan = scan + (moved * four_in if masked else moved)
                    entry = state[mode, :, lanes]
                    moved = onward_ref[mode, :, lanes] * entry
                    scan = scan + (moved * start_in if masked else moved)
                    state[mode, :, lanes] = jnp.broadcast_to(scan[SUB - 1 : SUB], (SUB, LANES))
                    running = jnp.where(rank == 0, entry, pltpu.roll(scan, 1, 0)) * scale_ref[mode, :, lanes]
                    decay = decay_ref[mode, :, lanes]
                    for t in range(STEPS):
                        running = running * decay
                        carried[t] = running if carried[t] is None else carried[t] + running
                for t in range(STEPS):
                    more = carried[t] * open_in[t] if masked else carried[t]
                    out_ref[tile, pl.ds(begin + t, SUB, stride=STEPS), :] = local[t] + more

        @pl.when(single)
        def _():
            tiles(False)

        @pl.when(jnp.logical_not(single))
        def _():
            tiles(True)

        return unused

    lax.fori_loop(0, blocks, one, 0)


def mix_kernel(turn, starts, arrived_ref, filtered_ref, out_ref, held, ready, sems):
    pieces = sems.shape[0]
    tiles, length, _ = filtered_ref.shape
    per = length // BLOCK // pieces
    compact(turn, starts, arrived_ref, held)

    def one(block, unused):
        rows = pl.ds(pl.multiple_of(block * BLOCK, BLOCK), BLOCK)
        for tile in range(tiles):
            ready[rows, pl.ds(tile * LANES, LANES)] = (held[tile, rows, :] * filtered_ref[tile, rows, :]).astype(BF16)
        return unused

    def copy(piece):
        rows = pl.ds(piece * per * BLOCK, per * BLOCK)
        return pltpu.make_async_copy(ready.at[rows, :], out_ref.at[rows, :], sems.at[piece])

    for piece in range(pieces):
        lax.fori_loop(piece * per, (piece + 1) * per, one, 0)
        copy(piece).start()
    for piece in range(pieces):
        copy(piece).wait()


def near_by(array):
    return pltpu.with_memory_space_constraint(array, pltpu.VMEM)


def local_call(kernel, outs, scalars, arrays, scratch, out_space=pltpu.VMEM):
    return pl.pallas_call(
        kernel,
        out_shape=outs,
        in_specs=[pl.BlockSpec(memory_space=pltpu.SMEM)] * len(scalars) + [pl.BlockSpec(memory_space=pltpu.VMEM)] * len(arrays),
        out_specs=jax.tree.map(lambda _: pl.BlockSpec(memory_space=out_space), outs),
        scratch_shapes=scratch,
        compiler_params=pltpu.CompilerParams(vmem_limit_bytes=24 << 20),
    )(*scalars, *[near_by(array) for array in arrays])


def passed_along(value, axis, steps):
    count = lax.axis_size(axis)
    return lax.ppermute(value, axis, [(source, source + steps) for source in range(count - steps)])


def shards(streams, load_counts, seg_ids, rates, residues, skip):
    capacity = streams.shape[0]
    groups = lax.axis_size("ch")
    channels, modes = rates.shape
    length = seg_ids.shape[0]
    blocks = length // BLOCK
    counts = load_counts[0]
    planes = jnp.transpose(streams, (1, 0, 2))
    order = [(rank - TURN) % groups for rank in range(groups)]
    signal_in = exchange(send((1, 2), planes, groups, channels, TURN, 8), order)
    query_out = send((0,), planes, groups, channels, TURN, 8)

    ending = jnp.sum(jnp.where(jnp.arange(groups)[:, None] >= jnp.arange(groups)[None, :], counts[None, :], 0), axis=1)
    starts = jnp.concatenate([jnp.zeros((1,), jnp.int32), ending]).astype(jnp.int32)
    bounds = jnp.sum((seg_ids[None, :] < jnp.arange(1, 4, dtype=jnp.int32)[:, None]).astype(jnp.int32), axis=1)

    rate = jnp.transpose(rates)
    gain = jnp.sqrt(-jnp.expm1(-2.0 * rate))
    scale = jnp.transpose(residues) * gain
    rank = jnp.arange(SUB, dtype=F32)[None, :, None]

    def power(exponent):
        return jnp.exp(-exponent * rate[:, None, :])

    flat = jnp.zeros((1, SUB, 1), F32)
    decay = power(1.0 + flat)
    weight = power((SUB - 1.0 - rank) * STEPS)
    leap = power(float(BLOCK) + flat)
    one_coef = jnp.where(rank >= 1, power(1.0 * STEPS + flat), 0.0)
    two_coef = jnp.where(rank >= 2, power(2.0 * STEPS + flat), 0.0)
    four_coef = jnp.where(rank >= 4, power(4.0 * STEPS + flat), 0.0)
    onward = power((rank + 1.0) * STEPS)
    scale_b = jnp.broadcast_to(scale[:, None, :], (modes, SUB, channels))
    lag = jnp.arange(STEPS, dtype=F32)[:, None, None]
    taps = jnp.sum(scale[None] * jnp.exp(-lag * rate[None]), axis=1)
    taps = taps + jnp.where(jnp.arange(STEPS)[:, None] == 0, skip[None, :], 0.0)
    taps_b = jnp.broadcast_to(taps[:, None, :], (STEPS, SUB, channels))
    span = jnp.exp(-float(length) * rate)

    prepared = (starts, bounds, decay, weight, leap, one_coef, two_coef, four_coef, onward, scale_b, taps_b, span)
    query_out, prepared = lax.optimization_barrier((query_out, prepared))
    starts, bounds, decay, weight, leap, one_coef, two_coef, four_coef, onward, scale_b, taps_b, span = prepared
    query_in = exchange(query_out, order)

    padded = (channels // LANES, length + capacity, LANES)
    signal, ends, passing = local_call(
        functools.partial(scan_kernel, TURN),
        (
            pltpu.VMEM(padded, F32),
            pltpu.VMEM((blocks, modes, SUB, channels), F32),
            pltpu.VMEM((modes + SUB, channels), F32),
        ),
        (starts, bounds),
        (signal_in, decay, weight, leap),
        [pltpu.VMEM((modes, SUB, channels), F32)],
    )
    near = passed_along(passing, "ctx", 1)
    far = passed_along(passing, "ctx", 2)
    farther = passed_along(passing, "ctx", 3)

    filtered = local_call(
        conv_kernel,
        pltpu.VMEM((channels // LANES, length, LANES), F32),
        (bounds,),
        (signal, ends, near, far, farther, decay, one_coef, two_coef, four_coef, onward, scale_b, taps_b, span),
        [pltpu.VMEM((modes, SUB, channels), F32)],
    )
    pieces = 4
    return local_call(
        functools.partial(mix_kernel, TURN),
        jax.ShapeDtypeStruct((length, channels), BF16),
        (starts,),
        (query_in, filtered),
        [
            pltpu.VMEM(padded, F32),
            pltpu.VMEM((length, channels), BF16),
            pltpu.SemaphoreType.DMA((pieces,)),
        ],
        pl.ANY,
    )


def solution(mesh):
    return jax.shard_map(
        shards,
        mesh=mesh,
        in_specs=(
            P(("ctx", "ch"), None, None),
            P("ctx", None),
            P("ctx"),
            P("ch", None),
            P("ch", None),
            P("ch"),
        ),
        out_specs=P("ctx", "ch"),
        check_vma=False,
    )
```

```python
import functools

import jax
import jax.numpy as jnp
from jax import lax
from jax.experimental import pallas as pl
from jax.experimental.pallas import tpu as pltpu
from jax.sharding import PartitionSpec as P

BLOCK = 128
STEPS = 16
LANES = 128
SUB = 8
TURN = 12
F32 = jnp.float32
BF16 = jnp.bfloat16


def send_kernel(planes, turn, streams_ref, out_ref, *scratch):
    held, ready, in_sems, out_sems = scratch[:-3], scratch[-3], scratch[-2], scratch[-1]
    pieces = in_sems.shape[1]
    groups, _, channels = out_ref.shape
    per = groups // pieces
    width = per * channels

    def load(plane, piece):
        columns = pl.ds(piece * width, width)
        return pltpu.make_async_copy(
            streams_ref.at[planes[plane], :, columns], held[plane].at[:, columns], in_sems.at[plane, piece]
        )

    def store(piece):
        goes = (piece * per + turn) % groups
        return pltpu.make_async_copy(ready.at[pl.ds(piece * per, per)], out_ref.at[pl.ds(goes, per)], out_sems.at[piece])

    for piece in range(pieces):
        for plane in range(len(planes)):
            load(plane, piece).start()
    for piece in range(pieces):
        for plane in range(len(planes)):
            load(plane, piece).wait()
        for part in range(piece * per, (piece + 1) * per):
            columns = pl.ds(part * channels, channels)
            value = held[0][:, columns]
            for other in held[1:]:
                value = value * other[:, columns]
            ready[part] = value
        store(piece).start()
    for piece in range(pieces):
        store(piece).wait()


def send(planes, streams, groups, channels, turn, pieces):
    rows = streams.shape[1]
    return pl.pallas_call(
        functools.partial(send_kernel, planes, turn),
        out_shape=pltpu.HBM((groups, rows, channels), BF16),
        in_specs=[pl.BlockSpec(memory_space=pltpu.HBM)],
        out_specs=pl.BlockSpec(memory_space=pltpu.HBM),
        scratch_shapes=[pltpu.VMEM((rows, groups * channels), BF16) for _ in planes]
        + [
            pltpu.VMEM((groups, rows, channels), BF16),
            pltpu.SemaphoreType.DMA((len(planes), pieces)),
            pltpu.SemaphoreType.DMA((pieces,)),
        ],
        compiler_params=pltpu.CompilerParams(vmem_limit_bytes=24 << 20),
    )(pltpu.with_memory_space_constraint(streams, pltpu.HBM))


def exchange(value, order):
    return lax.all_to_all(value, "ch", split_axis=0, concat_axis=0, axis_index_groups=[order], tiled=True)


def compact(turn, starts, arrived_ref, into_ref):
    sources, rows, channels = arrived_ref.shape

    def place(source, unused):
        begin = starts[source]
        slot = lax.rem(source + turn, sources)
        for part in range(0, rows, 2 * SUB):
            for tile in range(channels // LANES):
                piece = arrived_ref[slot, pl.ds(part, 2 * SUB), pl.ds(tile * LANES, LANES)].astype(F32)
                into_ref[tile, pl.ds(begin + part, SUB), :] = piece[:SUB]
                into_ref[tile, pl.ds(begin + part + SUB, SUB), :] = piece[SUB:]
        return unused

    lax.fori_loop(0, sources, place, 0)


def segment(position, bounds):
    total = (position >= bounds[0]).astype(jnp.int32)
    for bound in bounds[1:]:
        total = total + (position >= bound).astype(jnp.int32)
    return total


def scan_kernel(turn, starts, bounds, arrived_ref, decay_ref, weight_ref, leap_ref, signal_ref, ends_ref, passing_ref, carry):
    limits = [bounds[k] for k in range(3)]
    blocks, modes, _, channels = ends_ref.shape
    carry[...] = jnp.zeros_like(carry)
    rank = lax.broadcasted_iota(jnp.int32, (SUB, LANES), 0)
    compact(turn, starts, arrived_ref, signal_ref)

    def one(block, unused):
        begin = block * BLOCK
        first_id = segment(begin, limits)
        last_id = segment(begin + BLOCK - 1, limits)
        before_id = segment(begin - 1, limits)
        reach = segment(begin + rank * STEPS + STEPS - 1, limits) == last_id
        going = jnp.where(before_id == last_id, 1.0, 0.0)

        def tiles(masked):
            if masked:
                own = [segment(begin + rank * STEPS + t, limits) for t in range(STEPS)]
            for tile in range(channels // LANES):
                lanes = pl.ds(tile * LANES, LANES)
                rows = [signal_ref[tile, pl.ds(begin + t, SUB, stride=STEPS), :] for t in range(STEPS)]
                if masked:
                    rows = [jnp.where(o == own[-1], r, 0.0) for o, r in zip(own, rows)]
                for mode in range(modes):
                    decay = decay_ref[mode, :, lanes]
                    state = rows[0]
                    for t in range(1, STEPS):
                        state = decay * state + rows[t]
                    ends_ref[block, mode, :, lanes] = state
                    kept = weight_ref[mode, :, lanes] * state
                    if masked:
                        kept = jnp.where(reach, kept, 0.0)
                    carry[mode, :, lanes] = (going * leap_ref[mode, :, lanes]) * carry[mode, :, lanes] + kept

        @pl.when(first_id == last_id)
        def _():
            tiles(False)

        @pl.when(first_id != last_id)
        def _():
            tiles(True)

        return unused

    lax.fori_loop(0, blocks, one, 0)
    passing_ref[0:modes, :] = jnp.sum(carry[...], axis=1)
    line = lax.broadcasted_iota(jnp.int32, (SUB, channels), 0)
    ids = jnp.where(line == 0, segment(0, limits), segment(blocks * BLOCK - 1, limits))
    passing_ref[modes : modes + SUB, :] = ids.astype(F32)


def conv_kernel(
    bounds, signal_ref, ends_ref, near_ref, far_ref, farther_ref, decay_ref, one_ref, two_ref, four_ref, onward_ref, scale_ref, taps_ref, span_ref, out_ref, state
):
    limits = [bounds[k] for k in range(3)]
    blocks, modes, _, channels = ends_ref.shape
    start_id = segment(0, limits).astype(F32)

    def ids(ref):
        return ref[modes : modes + 1, :], ref[modes + 1 : modes + 2, :]

    near_first, near_last = ids(near_ref)
    far_first, far_last = ids(far_ref)
    _, farther_last = ids(farther_ref)
    through_far = jnp.where((far_first == far_last) & (far_first == farther_last), 1.0, 0.0)
    through_near = jnp.where((near_first == near_last) & (near_first == far_last), 1.0, 0.0)
    entering = jnp.where(near_last == start_id, 1.0, 0.0)
    span = span_ref[...]
    inside = far_ref[0:modes, :] + through_far * span * farther_ref[0:modes, :]
    inside = near_ref[0:modes, :] + through_near * span * inside
    inside = entering * inside
    for mode in range(modes):
        state[mode] = jnp.broadcast_to(inside[mode : mode + 1], (SUB, channels))

    rank = lax.broadcasted_iota(jnp.int32, (SUB, LANES), 0)

    def one(block, unused):
        begin = block * BLOCK
        last_id = segment(begin + BLOCK - 1, limits)
        before_id = segment(jnp.maximum(begin - 1, 0), limits)
        edge = segment(begin + rank * STEPS + STEPS - 1, limits)
        single = before_id == last_id

        def tiles(masked):
            if masked:
                one_in = jnp.where((rank >= 1) & (edge == pltpu.roll(edge, 1, 0)), 1.0, 0.0)
                two_in = jnp.where((rank >= 2) & (edge == pltpu.roll(edge, 2, 0)), 1.0, 0.0)
                four_in = jnp.where((rank >= 4) & (edge == pltpu.roll(edge, 4, 0)), 1.0, 0.0)
                start_in = jnp.where(edge == before_id, 1.0, 0.0)
                prior = jnp.where(rank == 0, before_id, pltpu.roll(edge, 1, 0))
                own = [segment(begin + rank * STEPS + t, limits) for t in range(STEPS)]
                open_in = [jnp.where(o == prior, 1.0, 0.0) for o in own]
            for tile in range(channels // LANES):
                lanes = pl.ds(tile * LANES, LANES)
                rows = [signal_ref[tile, pl.ds(begin + t, SUB, stride=STEPS), :] for t in range(STEPS)]
                local = []
                for t in range(STEPS):
                    total = taps_ref[0, :, lanes] * rows[t]
                    for u in range(t):
                        term = taps_ref[t - u, :, lanes] * rows[u]
                        if masked:
                            term = jnp.where(own[t] == own[u], term, 0.0)
                        total = total + term
                    local.append(total)
                carried = [None] * STEPS
                for mode in range(modes):
                    scan = ends_ref[block, mode, :, lanes]
                    moved = one_ref[mode, :, lanes] * pltpu.roll(scan, 1, 0)
                    scan = scan + (moved * one_in if masked else moved)
                    moved = two_ref[mode, :, lanes] * pltpu.roll(scan, 2, 0)
                    scan = scan + (moved * two_in if masked else moved)
                    moved = four_ref[mode, :, lanes] * pltpu.roll(scan, 4, 0)
                    scan = scan + (moved * four_in if masked else moved)
                    entry = state[mode, :, lanes]
                    moved = onward_ref[mode, :, lanes] * entry
                    scan = scan + (moved * start_in if masked else moved)
                    state[mode, :, lanes] = jnp.broadcast_to(scan[SUB - 1 : SUB], (SUB, LANES))
                    running = jnp.where(rank == 0, entry, pltpu.roll(scan, 1, 0)) * scale_ref[mode, :, lanes]
                    decay = decay_ref[mode, :, lanes]
                    for t in range(STEPS):
                        running = running * decay
                        carried[t] = running if carried[t] is None else carried[t] + running
                for t in range(STEPS):
                    more = carried[t] * open_in[t] if masked else carried[t]
                    out_ref[tile, pl.ds(begin + t, SUB, stride=STEPS), :] = local[t] + more

        @pl.when(single)
        def _():
            tiles(False)

        @pl.when(jnp.logical_not(single))
        def _():
            tiles(True)

        return unused

    lax.fori_loop(0, blocks, one, 0)


def mix_kernel(turn, starts, arrived_ref, filtered_ref, out_ref, held, ready, sems):
    pieces = sems.shape[0]
    tiles, length, _ = filtered_ref.shape
    per = length // BLOCK // pieces
    compact(turn, starts, arrived_ref, held)

    def one(block, unused):
        rows = pl.ds(pl.multiple_of(block * BLOCK, BLOCK), BLOCK)
        for tile in range(tiles):
            ready[rows, pl.ds(tile * LANES, LANES)] = (held[tile, rows, :] * filtered_ref[tile, rows, :]).astype(BF16)
        return unused

    def copy(piece):
        rows = pl.ds(piece * per * BLOCK, per * BLOCK)
        return pltpu.make_async_copy(ready.at[rows, :], out_ref.at[rows, :], sems.at[piece])

    for piece in range(pieces):
        lax.fori_loop(piece * per, (piece + 1) * per, one, 0)
        copy(piece).start()
    for piece in range(pieces):
        copy(piece).wait()


def near_by(array):
    return pltpu.with_memory_space_constraint(array, pltpu.VMEM)


def local_call(kernel, outs, scalars, arrays, scratch, out_space=pltpu.VMEM):
    return pl.pallas_call(
        kernel,
        out_shape=outs,
        in_specs=[pl.BlockSpec(memory_space=pltpu.SMEM)] * len(scalars) + [pl.BlockSpec(memory_space=pltpu.VMEM)] * len(arrays),
        out_specs=jax.tree.map(lambda _: pl.BlockSpec(memory_space=out_space), outs),
        scratch_shapes=scratch,
        compiler_params=pltpu.CompilerParams(vmem_limit_bytes=24 << 20),
    )(*scalars, *[near_by(array) for array in arrays])


def passed_along(value, axis, steps):
    count = lax.axis_size(axis)
    return lax.ppermute(value, axis, [(source, source + steps) for source in range(count - steps)])


def shards(streams, load_counts, seg_ids, rates, residues, skip):
    capacity = streams.shape[0]
    groups = lax.axis_size("ch")
    channels, modes = rates.shape
    length = seg_ids.shape[0]
    blocks = length // BLOCK
    counts = load_counts[0]
    planes = jnp.transpose(streams, (1, 0, 2))
    order = [(rank - TURN) % groups for rank in range(groups)]
    signal_in = exchange(send((1, 2), planes, groups, channels, TURN, 8), order)
    query_out = send((0,), planes, groups, channels, TURN, 8)

    ending = jnp.sum(jnp.where(jnp.arange(groups)[:, None] >= jnp.arange(groups)[None, :], counts[None, :], 0), axis=1)
    starts = jnp.concatenate([jnp.zeros((1,), jnp.int32), ending]).astype(jnp.int32)
    bounds = jnp.sum((seg_ids[None, :] < jnp.arange(1, 4, dtype=jnp.int32)[:, None]).astype(jnp.int32), axis=1)

    rate = jnp.transpose(rates)
    gain = jnp.sqrt(-jnp.expm1(-2.0 * rate))
    scale = jnp.transpose(residues) * gain
    rank = jnp.arange(SUB, dtype=F32)[None, :, None]

    def power(exponent):
        return jnp.exp(-exponent * rate[:, None, :])

    flat = jnp.zeros((1, SUB, 1), F32)
    decay = power(1.0 + flat)
    weight = power((SUB - 1.0 - rank) * STEPS)
    leap = power(float(BLOCK) + flat)
    one_coef = jnp.where(rank >= 1, power(1.0 * STEPS + flat), 0.0)
    two_coef = jnp.where(rank >= 2, power(2.0 * STEPS + flat), 0.0)
    four_coef = jnp.where(rank >= 4, power(4.0 * STEPS + flat), 0.0)
    onward = power((rank + 1.0) * STEPS)
    scale_b = jnp.broadcast_to(scale[:, None, :], (modes, SUB, channels))
    lag = jnp.arange(STEPS, dtype=F32)[:, None, None]
    taps = jnp.sum(scale[None] * jnp.exp(-lag * rate[None]), axis=1)
    taps = taps + jnp.where(jnp.arange(STEPS)[:, None] == 0, skip[None, :], 0.0)
    taps_b = jnp.broadcast_to(taps[:, None, :], (STEPS, SUB, channels))
    span = jnp.exp(-float(length) * rate)

    prepared = (starts, bounds, decay, weight, leap, one_coef, two_coef, four_coef, onward, scale_b, taps_b, span)
    query_out, prepared = lax.optimization_barrier((query_out, prepared))
    starts, bounds, decay, weight, leap, one_coef, two_coef, four_coef, onward, scale_b, taps_b, span = prepared
    query_in = exchange(query_out, order)

    padded = (channels // LANES, length + capacity, LANES)
    signal, ends, passing = local_call(
        functools.partial(scan_kernel, TURN),
        (
            pltpu.VMEM(padded, F32),
            pltpu.VMEM((blocks, modes, SUB, channels), F32),
            pltpu.VMEM((modes + SUB, channels), F32),
        ),
        (starts, bounds),
        (signal_in, decay, weight, leap),
        [pltpu.VMEM((modes, SUB, channels), F32)],
    )
    near = passed_along(passing, "ctx", 1)
    far = passed_along(passing, "ctx", 2)
    farther = passed_along(passing, "ctx", 3)

    filtered = local_call(
        conv_kernel,
        pltpu.VMEM((channels // LANES, length, LANES), F32),
        (bounds,),
        (signal, ends, near, far, farther, decay, one_coef, two_coef, four_coef, onward, scale_b, taps_b, span),
        [pltpu.VMEM((modes, SUB, channels), F32)],
    )
    pieces = 4
    return local_call(
        functools.partial(mix_kernel, TURN),
        jax.ShapeDtypeStruct((length, channels), BF16),
        (starts,),
        (query_in, filtered),
        [
            pltpu.VMEM(padded, F32),
            pltpu.VMEM((length, channels), BF16),
            pltpu.SemaphoreType.DMA((pieces,)),
        ],
        pl.ANY,
    )


def solution(mesh):
    return jax.shard_map(
        shards,
        mesh=mesh,
        in_specs=(
            P(("ctx", "ch"), None, None),
            P("ctx", None),
            P("ctx"),
            P("ch", None),
            P("ch", None),
            P("ch"),
        ),
        out_specs=P("ctx", "ch"),
        check_vma=False,
    )
```

```python
import functools

import jax
import jax.numpy as jnp
from jax import lax
from jax.experimental import pallas as pl
from jax.experimental.pallas import tpu as pltpu
from jax.sharding import PartitionSpec as P

BLOCK = 128
STEPS = 16
LANES = 128
SUB = 8
SIGNAL_TURN = 12
QUERY_TURN = 12
LOADS = 4
STORES = 8
F32 = jnp.float32
BF16 = jnp.bfloat16


def send_kernel(planes, turn, streams_ref, out_ref, *scratch):
    held, ready, in_sems, out_sems = scratch[:-3], scratch[-3], scratch[-2], scratch[-1]
    groups, _, channels = out_ref.shape
    width = groups * channels // LOADS
    per = groups // STORES

    def load(plane, piece):
        columns = pl.ds(piece * width, width)
        return pltpu.make_async_copy(
            streams_ref.at[planes[plane], :, columns], held[plane].at[:, columns], in_sems.at[plane, piece]
        )

    def store(piece):
        goes = (piece * per + turn) % groups
        return pltpu.make_async_copy(ready.at[pl.ds(piece * per, per)], out_ref.at[pl.ds(goes, per)], out_sems.at[piece])

    for piece in range(LOADS):
        for plane in range(len(planes)):
            load(plane, piece).start()
    for piece in range(STORES):
        if piece % (STORES // LOADS) == 0:
            for plane in range(len(planes)):
                load(plane, piece // (STORES // LOADS)).wait()
        for part in range(piece * per, (piece + 1) * per):
            columns = pl.ds(part * channels, channels)
            value = held[0][:, columns]
            for other in held[1:]:
                value = value * other[:, columns]
            ready[part] = value
        store(piece).start()
    for piece in range(STORES):
        store(piece).wait()


def send(planes, streams, groups, channels, turn):
    rows = streams.shape[1]
    return pl.pallas_call(
        functools.partial(send_kernel, planes, turn),
        out_shape=pltpu.HBM((groups, rows, channels), BF16),
        in_specs=[pl.BlockSpec(memory_space=pltpu.HBM)],
        out_specs=pl.BlockSpec(memory_space=pltpu.HBM),
        scratch_shapes=[pltpu.VMEM((rows, groups * channels), BF16) for _ in planes]
        + [
            pltpu.VMEM((groups, rows, channels), BF16),
            pltpu.SemaphoreType.DMA((len(planes), LOADS)),
            pltpu.SemaphoreType.DMA((STORES,)),
        ],
        compiler_params=pltpu.CompilerParams(vmem_limit_bytes=24 << 20),
    )(pltpu.with_memory_space_constraint(streams, pltpu.HBM))


def exchange(value, turn):
    groups = value.shape[0]
    order = [(rank - turn) % groups for rank in range(groups)]
    return lax.all_to_all(value, "ch", split_axis=0, concat_axis=0, axis_index_groups=[order], tiled=True)


def compact(turn, starts, arrived_ref, into_ref, first, last):
    sources, rows, channels = arrived_ref.shape

    def place(source, unused):
        begin = starts[source]
        slot = lax.rem(source + turn, sources)
        for part in range(0, rows, 2 * SUB):
            for tile in range(channels // LANES):
                piece = arrived_ref[slot, pl.ds(part, 2 * SUB), pl.ds(tile * LANES, LANES)].astype(F32)
                into_ref[tile, pl.ds(begin + part, SUB), :] = piece[:SUB]
                into_ref[tile, pl.ds(begin + part + SUB, SUB), :] = piece[SUB:]
        return unused

    lax.fori_loop(first, last, place, 0)


def segment(position, bounds):
    total = (position >= bounds[0]).astype(jnp.int32)
    for bound in bounds[1:]:
        total = total + (position >= bound).astype(jnp.int32)
    return total


def scan_kernel(turn, starts, bounds, arrived_ref, decay_ref, weight_ref, leap_ref, signal_ref, ends_ref, passing_ref, carry):
    limits = [bounds[k] for k in range(3)]
    blocks, modes, _, channels = ends_ref.shape
    carry[...] = jnp.zeros_like(carry)
    rank = lax.broadcasted_iota(jnp.int32, (SUB, LANES), 0)
    compact(turn, starts, arrived_ref, signal_ref, 0, arrived_ref.shape[0])

    def one(block, unused):
        begin = block * BLOCK
        first_id = segment(begin, limits)
        last_id = segment(begin + BLOCK - 1, limits)
        before_id = segment(begin - 1, limits)
        reach = segment(begin + rank * STEPS + STEPS - 1, limits) == last_id
        going = jnp.where(before_id == last_id, 1.0, 0.0)

        def tiles(masked):
            if masked:
                own = [segment(begin + rank * STEPS + t, limits) for t in range(STEPS)]
            for tile in range(channels // LANES):
                lanes = pl.ds(tile * LANES, LANES)
                rows = [signal_ref[tile, pl.ds(begin + t, SUB, stride=STEPS), :] for t in range(STEPS)]
                if masked:
                    rows = [jnp.where(o == own[-1], r, 0.0) for o, r in zip(own, rows)]
                for mode in range(modes):
                    decay = decay_ref[mode, :, lanes]
                    state = rows[0]
                    for t in range(1, STEPS):
                        state = decay * state + rows[t]
                    ends_ref[block, mode, :, lanes] = state
                    kept = weight_ref[mode, :, lanes] * state
                    if masked:
                        kept = jnp.where(reach, kept, 0.0)
                    carry[mode, :, lanes] = (going * leap_ref[mode, :, lanes]) * carry[mode, :, lanes] + kept

        @pl.when(first_id == last_id)
        def _():
            tiles(False)

        @pl.when(first_id != last_id)
        def _():
            tiles(True)

        return unused

    lax.fori_loop(0, blocks, one, 0)
    passing_ref[0:modes, :] = jnp.sum(carry[...], axis=1)
    line = lax.broadcasted_iota(jnp.int32, (SUB, channels), 0)
    ids = jnp.where(line == 0, segment(0, limits), segment(blocks * BLOCK - 1, limits))
    passing_ref[modes : modes + SUB, :] = ids.astype(F32)


def conv_kernel(
    bounds, signal_ref, ends_ref, near_ref, far_ref, farther_ref, decay_ref, one_ref, two_ref, four_ref, onward_ref, scale_ref, taps_ref, span_ref, out_ref, state
):
    limits = [bounds[k] for k in range(3)]
    blocks, modes, _, channels = ends_ref.shape
    start_id = segment(0, limits).astype(F32)

    def ids(ref):
        return ref[modes : modes + 1, :], ref[modes + 1 : modes + 2, :]

    near_first, near_last = ids(near_ref)
    far_first, far_last = ids(far_ref)
    _, farther_last = ids(farther_ref)
    through_far = jnp.where((far_first == far_last) & (far_first == farther_last), 1.0, 0.0)
    through_near = jnp.where((near_first == near_last) & (near_first == far_last), 1.0, 0.0)
    entering = jnp.where(near_last == start_id, 1.0, 0.0)
    span = span_ref[...]
    inside = far_ref[0:modes, :] + through_far * span * farther_ref[0:modes, :]
    inside = near_ref[0:modes, :] + through_near * span * inside
    inside = entering * inside
    for mode in range(modes):
        state[mode] = jnp.broadcast_to(inside[mode : mode + 1], (SUB, channels))

    rank = lax.broadcasted_iota(jnp.int32, (SUB, LANES), 0)

    def one(block, unused):
        begin = block * BLOCK
        last_id = segment(begin + BLOCK - 1, limits)
        before_id = segment(jnp.maximum(begin - 1, 0), limits)
        edge = segment(begin + rank * STEPS + STEPS - 1, limits)
        single = before_id == last_id

        def tiles(masked):
            if masked:
                one_in = jnp.where((rank >= 1) & (edge == pltpu.roll(edge, 1, 0)), 1.0, 0.0)
                two_in = jnp.where((rank >= 2) & (edge == pltpu.roll(edge, 2, 0)), 1.0, 0.0)
                four_in = jnp.where((rank >= 4) & (edge == pltpu.roll(edge, 4, 0)), 1.0, 0.0)
                start_in = jnp.where(edge == before_id, 1.0, 0.0)
                prior = jnp.where(rank == 0, before_id, pltpu.roll(edge, 1, 0))
                own = [segment(begin + rank * STEPS + t, limits) for t in range(STEPS)]
                open_in = [jnp.where(o == prior, 1.0, 0.0) for o in own]
            for tile in range(channels // LANES):
                lanes = pl.ds(tile * LANES, LANES)
                rows = [signal_ref[tile, pl.ds(begin + t, SUB, stride=STEPS), :] for t in range(STEPS)]
                local = []
                for t in range(STEPS):
                    total = taps_ref[0, :, lanes] * rows[t]
                    for u in range(t):
                        term = taps_ref[t - u, :, lanes] * rows[u]
                        if masked:
                            term = jnp.where(own[t] == own[u], term, 0.0)
                        total = total + term
                    local.append(total)
                carried = [None] * STEPS
                for mode in range(modes):
                    scan = ends_ref[block, mode, :, lanes]
                    moved = one_ref[mode, :, lanes] * pltpu.roll(scan, 1, 0)
                    scan = scan + (moved * one_in if masked else moved)
                    moved = two_ref[mode, :, lanes] * pltpu.roll(scan, 2, 0)
                    scan = scan + (moved * two_in if masked else moved)
                    moved = four_ref[mode, :, lanes] * pltpu.roll(scan, 4, 0)
                    scan = scan + (moved * four_in if masked else moved)
                    entry = state[mode, :, lanes]
                    moved = onward_ref[mode, :, lanes] * entry
                    scan = scan + (moved * start_in if masked else moved)
                    state[mode, :, lanes] = jnp.broadcast_to(scan[SUB - 1 : SUB], (SUB, LANES))
                    running = jnp.where(rank == 0, entry, pltpu.roll(scan, 1, 0)) * scale_ref[mode, :, lanes]
                    decay = decay_ref[mode, :, lanes]
                    for t in range(STEPS):
                        running = running * decay
                        carried[t] = running if carried[t] is None else carried[t] + running
                for t in range(STEPS):
                    more = carried[t] * open_in[t] if masked else carried[t]
                    out_ref[tile, pl.ds(begin + t, SUB, stride=STEPS), :] = local[t] + more

        @pl.when(single)
        def _():
            tiles(False)

        @pl.when(jnp.logical_not(single))
        def _():
            tiles(True)

        return unused

    lax.fori_loop(0, blocks, one, 0)


def mix_kernel(turn, starts, arrived_ref, filtered_ref, out_ref, landed, held, ready, in_sems, out_sems):
    tiles, length, _ = filtered_ref.shape
    pieces = in_sems.shape[0]
    sources = arrived_ref.shape[0]
    per = sources // pieces

    def load(piece):
        slots = pl.ds((piece * per + turn) % sources, per)
        return pltpu.make_async_copy(arrived_ref.at[slots], landed.at[slots], in_sems.at[piece])

    def store(block):
        rows = pl.ds(pl.multiple_of(block * BLOCK, BLOCK), BLOCK)
        return pltpu.make_async_copy(ready.at[rows, :], out_ref.at[rows, :], out_sems.at[block])

    def finish(block, unused):
        rows = pl.ds(pl.multiple_of(block * BLOCK, BLOCK), BLOCK)
        for tile in range(tiles):
            ready[rows, pl.ds(tile * LANES, LANES)] = (held[tile, rows, :] * filtered_ref[tile, rows, :]).astype(BF16)
        store(block).start()
        return unused

    for piece in range(pieces):
        load(piece).start()
    complete = 0
    for piece in range(pieces):
        load(piece).wait()
        compact(turn, starts, landed, held, piece * per, (piece + 1) * per)
        reached = starts[(piece + 1) * per] >> 7
        lax.fori_loop(complete, reached, finish, 0)
        complete = reached
    for block in range(length // BLOCK):
        store(block).wait()


def near_by(array):
    return pltpu.with_memory_space_constraint(array, pltpu.VMEM)


def local_call(kernel, outs, scalars, arrays, scratch):
    spaces = (pltpu.SMEM,) * len(scalars) + (pltpu.VMEM,) * len(arrays)
    return pl.pallas_call(
        kernel,
        out_shape=outs,
        in_specs=[pl.BlockSpec(memory_space=space) for space in spaces],
        out_specs=jax.tree.map(lambda _: pl.BlockSpec(memory_space=pltpu.VMEM), outs),
        scratch_shapes=scratch,
        compiler_params=pltpu.CompilerParams(vmem_limit_bytes=24 << 20),
    )(*scalars, *[near_by(array) for array in arrays])


def passed_along(value, axis, steps):
    count = lax.axis_size(axis)
    return lax.ppermute(value, axis, [(source, source + steps) for source in range(count - steps)])


def shards(streams, load_counts, seg_ids, rates, residues, skip):
    capacity = streams.shape[0]
    groups = lax.axis_size("ch")
    channels, modes = rates.shape
    length = seg_ids.shape[0]
    blocks = length // BLOCK
    counts = load_counts[0]
    planes = jnp.transpose(streams, (1, 0, 2))
    signal_in = exchange(send((1, 2), planes, groups, channels, SIGNAL_TURN), SIGNAL_TURN)
    query_out = send((0,), planes, groups, channels, QUERY_TURN)

    ending = jnp.sum(jnp.where(jnp.arange(groups)[:, None] >= jnp.arange(groups)[None, :], counts[None, :], 0), axis=1)
    starts = jnp.concatenate([jnp.zeros((1,), jnp.int32), ending]).astype(jnp.int32)
    bounds = jnp.sum((seg_ids[None, :] < jnp.arange(1, 4, dtype=jnp.int32)[:, None]).astype(jnp.int32), axis=1)

    rate = jnp.transpose(rates)
    gain = jnp.sqrt(-jnp.expm1(-2.0 * rate))
    scale = jnp.transpose(residues) * gain
    rank = jnp.arange(SUB, dtype=F32)[None, :, None]

    def power(exponent):
        return jnp.exp(-exponent * rate[:, None, :])

    flat = jnp.zeros((1, SUB, 1), F32)
    decay = power(1.0 + flat)
    weight = power((SUB - 1.0 - rank) * STEPS)
    leap = power(float(BLOCK) + flat)
    one_coef = jnp.where(rank >= 1, power(1.0 * STEPS + flat), 0.0)
    two_coef = jnp.where(rank >= 2, power(2.0 * STEPS + flat), 0.0)
    four_coef = jnp.where(rank >= 4, power(4.0 * STEPS + flat), 0.0)
    onward = power((rank + 1.0) * STEPS)
    scale_b = jnp.broadcast_to(scale[:, None, :], (modes, SUB, channels))
    lag = jnp.arange(STEPS, dtype=F32)[:, None, None]
    taps = jnp.sum(scale[None] * jnp.exp(-lag * rate[None]), axis=1)
    taps = taps + jnp.where(jnp.arange(STEPS)[:, None] == 0, skip[None, :], 0.0)
    taps_b = jnp.broadcast_to(taps[:, None, :], (STEPS, SUB, channels))
    span = jnp.exp(-float(length) * rate)

    prepared = (starts, bounds, decay, weight, leap, one_coef, two_coef, four_coef, onward, scale_b, taps_b, span)
    query_out, prepared = lax.optimization_barrier((query_out, prepared))
    starts, bounds, decay, weight, leap, one_coef, two_coef, four_coef, onward, scale_b, taps_b, span = prepared
    query_in = exchange(query_out, QUERY_TURN)

    padded = (channels // LANES, length + capacity, LANES)
    signal, ends, passing = local_call(
        functools.partial(scan_kernel, SIGNAL_TURN),
        (
            pltpu.VMEM(padded, F32),
            pltpu.VMEM((blocks, modes, SUB, channels), F32),
            pltpu.VMEM((modes + SUB, channels), F32),
        ),
        (starts, bounds),
        (signal_in, decay, weight, leap),
        [pltpu.VMEM((modes, SUB, channels), F32)],
    )
    near = passed_along(passing, "ctx", 1)
    far = passed_along(passing, "ctx", 2)
    farther = passed_along(passing, "ctx", 3)

    filtered = local_call(
        conv_kernel,
        pltpu.VMEM((channels // LANES, length, LANES), F32),
        (bounds,),
        (signal, ends, near, far, farther, decay, one_coef, two_coef, four_coef, onward, scale_b, taps_b, span),
        [pltpu.VMEM((modes, SUB, channels), F32)],
    )
    pieces = 8
    return pl.pallas_call(
        functools.partial(mix_kernel, QUERY_TURN),
        out_shape=pltpu.HBM((length, channels), BF16),
        in_specs=[pl.BlockSpec(memory_space=space) for space in (pltpu.SMEM, pltpu.HBM, pltpu.VMEM)],
        out_specs=pl.BlockSpec(memory_space=pltpu.HBM),
        scratch_shapes=[
            pltpu.VMEM((groups, capacity, channels), BF16),
            pltpu.VMEM(padded, F32),
            pltpu.VMEM((length, channels), BF16),
            pltpu.SemaphoreType.DMA((pieces,)),
            pltpu.SemaphoreType.DMA((blocks,)),
        ],
        compiler_params=pltpu.CompilerParams(vmem_limit_bytes=24 << 20),
    )(starts, pltpu.with_memory_space_constraint(query_in, pltpu.HBM), near_by(filtered))


def solution(mesh):
    return jax.shard_map(
        shards,
        mesh=mesh,
        in_specs=(
            P(("ctx", "ch"), None, None),
            P("ctx", None),
            P("ctx"),
            P("ch", None),
            P("ch", None),
            P("ch"),
        ),
        out_specs=P("ctx", "ch"),
        check_vma=False,
    )
```

```python
import functools

import jax
import jax.numpy as jnp
from jax import lax
from jax.experimental import pallas as pl
from jax.experimental.pallas import tpu as pltpu
from jax.sharding import PartitionSpec as P

BLOCK = 128
STEPS = 16
LANES = 128
SUB = 8
SIGNAL_TURN = 12
QUERY_TURN = 12
LOADS = 4
STORES = 8
PIECES = 8
F32 = jnp.float32
BF16 = jnp.bfloat16


def send_kernel(planes, turn, streams_ref, out_ref, *scratch):
    held, ready, in_sems, out_sems = scratch[:-3], scratch[-3], scratch[-2], scratch[-1]
    groups, _, channels = out_ref.shape
    width = groups * channels // LOADS
    per = groups // STORES

    def load(plane, piece):
        columns = pl.ds(piece * width, width)
        return pltpu.make_async_copy(
            streams_ref.at[planes[plane], :, columns], held[plane].at[:, columns], in_sems.at[plane, piece]
        )

    def store(piece):
        goes = (piece * per + turn) % groups
        return pltpu.make_async_copy(ready.at[pl.ds(piece * per, per)], out_ref.at[pl.ds(goes, per)], out_sems.at[piece])

    for piece in range(LOADS):
        for plane in range(len(planes)):
            load(plane, piece).start()
    for piece in range(STORES):
        if piece % (STORES // LOADS) == 0:
            for plane in range(len(planes)):
                load(plane, piece // (STORES // LOADS)).wait()
        for part in range(piece * per, (piece + 1) * per):
            columns = pl.ds(part * channels, channels)
            value = held[0][:, columns]
            for other in held[1:]:
                value = value * other[:, columns]
            ready[part] = value
        store(piece).start()
    for piece in range(STORES):
        store(piece).wait()


def send(planes, streams, groups, channels, turn):
    rows = streams.shape[1]
    return pl.pallas_call(
        functools.partial(send_kernel, planes, turn),
        out_shape=pltpu.HBM((groups, rows, channels), BF16),
        in_specs=[pl.BlockSpec(memory_space=pltpu.HBM)],
        out_specs=pl.BlockSpec(memory_space=pltpu.HBM),
        scratch_shapes=[pltpu.VMEM((rows, groups * channels), BF16) for _ in planes]
        + [
            pltpu.VMEM((groups, rows, channels), BF16),
            pltpu.SemaphoreType.DMA((len(planes), LOADS)),
            pltpu.SemaphoreType.DMA((STORES,)),
        ],
        compiler_params=pltpu.CompilerParams(vmem_limit_bytes=24 << 20),
    )(far_off(streams))


def exchange(value, turn):
    groups = value.shape[0]
    order = [(rank - turn) % groups for rank in range(groups)]
    return lax.all_to_all(value, "ch", split_axis=0, concat_axis=0, axis_index_groups=[order], tiled=True)


def compact(turn, starts, arrived_ref, into_ref, first, last):
    sources, rows, channels = arrived_ref.shape

    def place(source, unused):
        begin = starts[source]
        slot = lax.rem(source + turn, sources)
        for part in range(0, rows, 2 * SUB):
            for tile in range(channels // LANES):
                piece = arrived_ref[slot, pl.ds(part, 2 * SUB), pl.ds(tile * LANES, LANES)].astype(F32)
                into_ref[tile, pl.ds(begin + part, SUB), :] = piece[:SUB]
                into_ref[tile, pl.ds(begin + part + SUB, SUB), :] = piece[SUB:]
        return unused

    lax.fori_loop(first, last, place, 0)


def segment(position, bounds):
    total = (position >= bounds[0]).astype(jnp.int32)
    for bound in bounds[1:]:
        total = total + (position >= bound).astype(jnp.int32)
    return total


def scan_kernel(turn, starts, bounds, arrived_ref, decay_ref, weight_ref, leap_ref, signal_ref, ends_ref, passing_ref, carry):
    limits = [bounds[k] for k in range(3)]
    blocks, modes, _, channels = ends_ref.shape
    carry[...] = jnp.zeros_like(carry)
    rank = lax.broadcasted_iota(jnp.int32, (SUB, LANES), 0)
    compact(turn, starts, arrived_ref, signal_ref, 0, arrived_ref.shape[0])

    def one(block, unused):
        begin = block * BLOCK
        first_id = segment(begin, limits)
        last_id = segment(begin + BLOCK - 1, limits)
        before_id = segment(begin - 1, limits)
        reach = segment(begin + rank * STEPS + STEPS - 1, limits) == last_id
        going = jnp.where(before_id == last_id, 1.0, 0.0)

        def tiles(masked):
            if masked:
                own = [segment(begin + rank * STEPS + t, limits) for t in range(STEPS)]
            for tile in range(channels // LANES):
                lanes = pl.ds(tile * LANES, LANES)
                rows = [signal_ref[tile, pl.ds(begin + t, SUB, stride=STEPS), :] for t in range(STEPS)]
                if masked:
                    rows = [jnp.where(o == own[-1], r, 0.0) for o, r in zip(own, rows)]
                for mode in range(modes):
                    decay = decay_ref[mode, :, lanes]
                    state = rows[0]
                    for t in range(1, STEPS):
                        state = decay * state + rows[t]
                    ends_ref[block, mode, :, lanes] = state
                    kept = weight_ref[mode, :, lanes] * state
                    if masked:
                        kept = jnp.where(reach, kept, 0.0)
                    carry[mode, :, lanes] = (going * leap_ref[mode, :, lanes]) * carry[mode, :, lanes] + kept

        @pl.when(first_id == last_id)
        def _():
            tiles(False)

        @pl.when(first_id != last_id)
        def _():
            tiles(True)

        return unused

    lax.fori_loop(0, blocks, one, 0)
    passing_ref[0:modes, :] = jnp.sum(carry[...], axis=1)
    line = lax.broadcasted_iota(jnp.int32, (SUB, channels), 0)
    ids = jnp.where(line == 0, segment(0, limits), segment(blocks * BLOCK - 1, limits))
    passing_ref[modes : modes + SUB, :] = ids.astype(F32)


def conv_kernel(
    bounds, signal_ref, ends_ref, near_ref, far_ref, farther_ref, decay_ref, one_ref, two_ref, four_ref, onward_ref, scale_ref, taps_ref, span_ref, out_ref, state
):
    limits = [bounds[k] for k in range(3)]
    blocks, modes, _, channels = ends_ref.shape
    start_id = segment(0, limits).astype(F32)

    def ids(ref):
        return ref[modes : modes + 1, :], ref[modes + 1 : modes + 2, :]

    near_first, near_last = ids(near_ref)
    far_first, far_last = ids(far_ref)
    _, farther_last = ids(farther_ref)
    through_far = jnp.where((far_first == far_last) & (far_first == farther_last), 1.0, 0.0)
    through_near = jnp.where((near_first == near_last) & (near_first == far_last), 1.0, 0.0)
    entering = jnp.where(near_last == start_id, 1.0, 0.0)
    span = span_ref[...]
    inside = far_ref[0:modes, :] + through_far * span * farther_ref[0:modes, :]
    inside = near_ref[0:modes, :] + through_near * span * inside
    inside = entering * inside
    for mode in range(modes):
        state[mode] = jnp.broadcast_to(inside[mode : mode + 1], (SUB, channels))

    rank = lax.broadcasted_iota(jnp.int32, (SUB, LANES), 0)

    def one(block, unused):
        begin = block * BLOCK
        last_id = segment(begin + BLOCK - 1, limits)
        before_id = segment(jnp.maximum(begin - 1, 0), limits)
        edge = segment(begin + rank * STEPS + STEPS - 1, limits)
        single = before_id == last_id

        def tiles(masked):
            if masked:
                one_in = jnp.where((rank >= 1) & (edge == pltpu.roll(edge, 1, 0)), 1.0, 0.0)
                two_in = jnp.where((rank >= 2) & (edge == pltpu.roll(edge, 2, 0)), 1.0, 0.0)
                four_in = jnp.where((rank >= 4) & (edge == pltpu.roll(edge, 4, 0)), 1.0, 0.0)
                start_in = jnp.where(edge == before_id, 1.0, 0.0)
                prior = jnp.where(rank == 0, before_id, pltpu.roll(edge, 1, 0))
                own = [segment(begin + rank * STEPS + t, limits) for t in range(STEPS)]
                open_in = [jnp.where(o == prior, 1.0, 0.0) for o in own]
            for tile in range(channels // LANES):
                lanes = pl.ds(tile * LANES, LANES)
                rows = [signal_ref[tile, pl.ds(begin + t, SUB, stride=STEPS), :] for t in range(STEPS)]
                local = []
                for t in range(STEPS):
                    total = taps_ref[0, :, lanes] * rows[t]
                    for u in range(t):
                        term = taps_ref[t - u, :, lanes] * rows[u]
                        if masked:
                            term = jnp.where(own[t] == own[u], term, 0.0)
                        total = total + term
                    local.append(total)
                carried = [None] * STEPS
                for mode in range(modes):
                    scan = ends_ref[block, mode, :, lanes]
                    moved = one_ref[mode, :, lanes] * pltpu.roll(scan, 1, 0)
                    scan = scan + (moved * one_in if masked else moved)
                    moved = two_ref[mode, :, lanes] * pltpu.roll(scan, 2, 0)
                    scan = scan + (moved * two_in if masked else moved)
                    moved = four_ref[mode, :, lanes] * pltpu.roll(scan, 4, 0)
                    scan = scan + (moved * four_in if masked else moved)
                    entry = state[mode, :, lanes]
                    moved = onward_ref[mode, :, lanes] * entry
                    scan = scan + (moved * start_in if masked else moved)
                    state[mode, :, lanes] = jnp.broadcast_to(scan[SUB - 1 : SUB], (SUB, LANES))
                    running = jnp.where(rank == 0, entry, pltpu.roll(scan, 1, 0)) * scale_ref[mode, :, lanes]
                    decay = decay_ref[mode, :, lanes]
                    for t in range(STEPS):
                        running = running * decay
                        carried[t] = running if carried[t] is None else carried[t] + running
                for t in range(STEPS):
                    more = carried[t] * open_in[t] if masked else carried[t]
                    out_ref[tile, pl.ds(begin + t, SUB, stride=STEPS), :] = local[t] + more

        @pl.when(single)
        def _():
            tiles(False)

        @pl.when(jnp.logical_not(single))
        def _():
            tiles(True)

        return unused

    lax.fori_loop(0, blocks, one, 0)


def mix_kernel(turn, starts_ref, arrived_ref, filtered_ref, out_ref, starts, landed, held, ready, table_sem, in_sems, out_sems):
    tiles, length, _ = filtered_ref.shape
    pieces = in_sems.shape[0]
    sources = arrived_ref.shape[0]
    per = sources // pieces

    def load(piece):
        slots = pl.ds((piece * per + turn) % sources, per)
        return pltpu.make_async_copy(arrived_ref.at[slots], landed.at[slots], in_sems.at[piece])

    def store(block):
        rows = pl.ds(pl.multiple_of(block * BLOCK, BLOCK), BLOCK)
        return pltpu.make_async_copy(ready.at[rows, :], out_ref.at[rows, :], out_sems.at[block])

    def finish(block, unused):
        rows = pl.ds(pl.multiple_of(block * BLOCK, BLOCK), BLOCK)
        for tile in range(tiles):
            ready[rows, pl.ds(tile * LANES, LANES)] = (held[tile, rows, :] * filtered_ref[tile, rows, :]).astype(BF16)
        store(block).start()
        return unused

    table = pltpu.make_async_copy(starts_ref, starts, table_sem)
    table.start()
    for piece in range(pieces):
        load(piece).start()
    table.wait()
    complete = 0
    for piece in range(pieces):
        load(piece).wait()
        compact(turn, starts, landed, held, piece * per, (piece + 1) * per)
        reached = starts[(piece + 1) * per] >> 7
        lax.fori_loop(complete, reached, finish, 0)
        complete = reached
    for block in range(length // BLOCK):
        store(block).wait()


def near_by(array):
    return pltpu.with_memory_space_constraint(array, pltpu.VMEM)


def far_off(array):
    return pltpu.with_memory_space_constraint(array, pltpu.HBM)


def local_call(kernel, outs, scalars, arrays, scratch):
    spaces = (pltpu.SMEM,) * len(scalars) + (pltpu.VMEM,) * len(arrays)
    return pl.pallas_call(
        kernel,
        out_shape=outs,
        in_specs=[pl.BlockSpec(memory_space=space) for space in spaces],
        out_specs=jax.tree.map(lambda _: pl.BlockSpec(memory_space=pltpu.VMEM), outs),
        scratch_shapes=scratch,
        compiler_params=pltpu.CompilerParams(vmem_limit_bytes=24 << 20),
    )(*scalars, *[near_by(array) for array in arrays])


def passed_along(value, axis, steps):
    count = lax.axis_size(axis)
    return lax.ppermute(value, axis, [(source, source + steps) for source in range(count - steps)])


def shards(streams, load_counts, seg_ids, rates, residues, skip):
    capacity = streams.shape[0]
    groups = lax.axis_size("ch")
    channels, modes = rates.shape
    length = seg_ids.shape[0]
    blocks = length // BLOCK
    counts = load_counts[0]
    planes = jnp.transpose(streams, (1, 0, 2))
    signal_in = exchange(send((1, 2), planes, groups, channels, SIGNAL_TURN), SIGNAL_TURN)
    query_out = send((0,), planes, groups, channels, QUERY_TURN)

    ending = jnp.sum(jnp.where(jnp.arange(groups)[:, None] >= jnp.arange(groups)[None, :], counts[None, :], 0), axis=1)
    starts = jnp.concatenate([jnp.zeros((1,), jnp.int32), ending, jnp.zeros((BLOCK - 1 - groups,), jnp.int32)])
    starts = starts.astype(jnp.int32)
    bounds = jnp.sum((seg_ids[None, :] < jnp.arange(1, 4, dtype=jnp.int32)[:, None]).astype(jnp.int32), axis=1)

    rate = jnp.transpose(rates)
    gain = jnp.sqrt(-jnp.expm1(-2.0 * rate))
    scale = jnp.transpose(residues) * gain
    rank = jnp.arange(SUB, dtype=F32)[None, :, None]

    def power(exponent):
        return jnp.exp(-exponent * rate[:, None, :])

    flat = jnp.zeros((1, SUB, 1), F32)
    decay = power(1.0 + flat)
    weight = power((SUB - 1.0 - rank) * STEPS)
    leap = power(float(BLOCK) + flat)
    one_coef = jnp.where(rank >= 1, power(1.0 * STEPS + flat), 0.0)
    two_coef = jnp.where(rank >= 2, power(2.0 * STEPS + flat), 0.0)
    four_coef = jnp.where(rank >= 4, power(4.0 * STEPS + flat), 0.0)
    onward = power((rank + 1.0) * STEPS)
    scale_b = jnp.broadcast_to(scale[:, None, :], (modes, SUB, channels))
    lag = jnp.arange(STEPS, dtype=F32)[:, None, None]
    taps = jnp.sum(scale[None] * jnp.exp(-lag * rate[None]), axis=1)
    taps = taps + jnp.where(jnp.arange(STEPS)[:, None] == 0, skip[None, :], 0.0)
    taps_b = jnp.broadcast_to(taps[:, None, :], (STEPS, SUB, channels))
    span = jnp.exp(-float(length) * rate)

    prepared = (starts, bounds, decay, weight, leap, one_coef, two_coef, four_coef, onward, scale_b, taps_b, span)
    query_out, prepared = lax.optimization_barrier((query_out, prepared))
    starts, bounds, decay, weight, leap, one_coef, two_coef, four_coef, onward, scale_b, taps_b, span = prepared
    query_in = exchange(query_out, QUERY_TURN)

    padded = (channels // LANES, length + capacity, LANES)
    signal, ends, passing = local_call(
        functools.partial(scan_kernel, SIGNAL_TURN),
        (
            pltpu.VMEM(padded, F32),
            pltpu.VMEM((blocks, modes, SUB, channels), F32),
            pltpu.VMEM((modes + SUB, channels), F32),
        ),
        (starts, bounds),
        (signal_in, decay, weight, leap),
        [pltpu.VMEM((modes, SUB, channels), F32)],
    )
    near = passed_along(passing, "ctx", 1)
    far = passed_along(passing, "ctx", 2)
    farther = passed_along(passing, "ctx", 3)

    filtered = local_call(
        conv_kernel,
        pltpu.VMEM((channels // LANES, length, LANES), F32),
        (bounds,),
        (signal, ends, near, far, farther, decay, one_coef, two_coef, four_coef, onward, scale_b, taps_b, span),
        [pltpu.VMEM((modes, SUB, channels), F32)],
    )
    pieces = PIECES
    return pl.pallas_call(
        functools.partial(mix_kernel, QUERY_TURN),
        out_shape=pltpu.HBM((length, channels), BF16),
        in_specs=[pl.BlockSpec(memory_space=space) for space in (pltpu.HBM, pltpu.HBM, pltpu.VMEM)],
        out_specs=pl.BlockSpec(memory_space=pltpu.HBM),
        scratch_shapes=[
            pltpu.SMEM(starts.shape, jnp.int32),
            pltpu.VMEM((groups, capacity, channels), BF16),
            pltpu.VMEM(padded, F32),
            pltpu.VMEM((length, channels), BF16),
            pltpu.SemaphoreType.DMA,
            pltpu.SemaphoreType.DMA((pieces,)),
            pltpu.SemaphoreType.DMA((blocks,)),
        ],
        compiler_params=pltpu.CompilerParams(vmem_limit_bytes=24 << 20),
    )(far_off(starts), far_off(query_in), near_by(filtered))


def solution(mesh):
    return jax.shard_map(
        shards,
        mesh=mesh,
        in_specs=(
            P(("ctx", "ch"), None, None),
            P("ctx", None),
            P("ctx"),
            P("ch", None),
            P("ch", None),
            P("ch"),
        ),
        out_specs=P("ctx", "ch"),
        check_vma=False,
    )
```

```python
import functools

import jax
import jax.numpy as jnp
from jax import lax
from jax.experimental import pallas as pl
from jax.experimental.pallas import tpu as pltpu
from jax.sharding import PartitionSpec as P

BLOCK = 128
STEPS = 16
LANES = 128
SUB = 8
SIGNAL_CHIPS = (10, 11, 12, 13, 14, 15, 0, 1, 2, 3, 4, 5, 6, 7, 8, 9)
QUERY_CHIPS = (10, 11, 14, 15, 12, 9, 13, 1, 7, 3, 0, 5, 2, 4, 8, 6)
LOADS = 4
F32 = jnp.float32
BF16 = jnp.bfloat16


def send_kernel(planes, chips, streams_ref, out_ref, *scratch):
    held, ready, in_sems, out_sems = scratch[:-3], scratch[-3], scratch[-2], scratch[-1]
    groups, _, channels = out_ref.shape
    width = groups * channels // LOADS
    per = groups // len(chips)
    each = len(chips) // LOADS

    def load(plane, piece):
        columns = pl.ds(piece * width, width)
        return pltpu.make_async_copy(
            streams_ref.at[planes[plane], :, columns], held[plane].at[:, columns], in_sems.at[plane, piece]
        )

    def store(piece):
        goes = pl.ds(chips.index(piece) * per, per)
        return pltpu.make_async_copy(ready.at[pl.ds(piece * per, per)], out_ref.at[goes], out_sems.at[piece])

    for piece in range(LOADS):
        for plane in range(len(planes)):
            load(plane, piece).start()
    for piece in range(len(chips)):
        if piece % each == 0:
            for plane in range(len(planes)):
                load(plane, piece // each).wait()
        for part in range(piece * per, (piece + 1) * per):
            columns = pl.ds(part * channels, channels)
            value = held[0][:, columns]
            for other in held[1:]:
                value = value * other[:, columns]
            ready[part] = value
        store(piece).start()
    for piece in range(len(chips)):
        store(piece).wait()


def send(planes, streams, groups, channels, chips):
    rows = streams.shape[1]
    return pl.pallas_call(
        functools.partial(send_kernel, planes, chips),
        out_shape=pltpu.HBM((groups, rows, channels), BF16),
        in_specs=[pl.BlockSpec(memory_space=pltpu.HBM)],
        out_specs=pl.BlockSpec(memory_space=pltpu.HBM),
        scratch_shapes=[pltpu.VMEM((rows, groups * channels), BF16) for _ in planes]
        + [
            pltpu.VMEM((groups, rows, channels), BF16),
            pltpu.SemaphoreType.DMA((len(planes), LOADS)),
            pltpu.SemaphoreType.DMA((len(chips),)),
        ],
        compiler_params=pltpu.CompilerParams(vmem_limit_bytes=24 << 20),
    )(far_off(streams))


def exchange(value, chips):
    per = value.shape[0] // len(chips)
    order = [chip * per + core for chip in chips for core in range(per)]
    return lax.all_to_all(value, "ch", split_axis=0, concat_axis=0, axis_index_groups=[order], tiled=True)


def compact(chips, starts, arrived_ref, into_ref, first, last):
    groups, rows, channels = arrived_ref.shape
    per = groups // len(chips)
    for chip in range(first, last):
        slots = chips.index(chip) * per

        def place(core, unused, chip=chip, slots=slots):
            begin = starts[chip * per + core]
            for part in range(0, rows, 2 * SUB):
                for tile in range(channels // LANES):
                    piece = arrived_ref[slots + core, pl.ds(part, 2 * SUB), pl.ds(tile * LANES, LANES)].astype(F32)
                    into_ref[tile, pl.ds(begin + part, SUB), :] = piece[:SUB]
                    into_ref[tile, pl.ds(begin + part + SUB, SUB), :] = piece[SUB:]
            return unused

        lax.fori_loop(0, per, place, 0)


def segment(position, bounds):
    total = (position >= bounds[0]).astype(jnp.int32)
    for bound in bounds[1:]:
        total = total + (position >= bound).astype(jnp.int32)
    return total


def scan_kernel(chips, starts, bounds, arrived_ref, decay_ref, weight_ref, leap_ref, signal_ref, ends_ref, passing_ref, carry):
    limits = [bounds[k] for k in range(3)]
    blocks, modes, _, channels = ends_ref.shape
    carry[...] = jnp.zeros_like(carry)
    rank = lax.broadcasted_iota(jnp.int32, (SUB, LANES), 0)
    compact(chips, starts, arrived_ref, signal_ref, 0, len(chips))

    def one(block, unused):
        begin = block * BLOCK
        first_id = segment(begin, limits)
        last_id = segment(begin + BLOCK - 1, limits)
        before_id = segment(begin - 1, limits)
        reach = segment(begin + rank * STEPS + STEPS - 1, limits) == last_id
        going = jnp.where(before_id == last_id, 1.0, 0.0)

        def tiles(masked):
            if masked:
                own = [segment(begin + rank * STEPS + t, limits) for t in range(STEPS)]
            for tile in range(channels // LANES):
                lanes = pl.ds(tile * LANES, LANES)
                rows = [signal_ref[tile, pl.ds(begin + t, SUB, stride=STEPS), :] for t in range(STEPS)]
                if masked:
                    rows = [jnp.where(o == own[-1], r, 0.0) for o, r in zip(own, rows)]
                for mode in range(modes):
                    decay = decay_ref[mode, :, lanes]
                    state = rows[0]
                    for t in range(1, STEPS):
                        state = decay * state + rows[t]
                    ends_ref[block, mode, :, lanes] = state
                    kept = weight_ref[mode, :, lanes] * state
                    if masked:
                        kept = jnp.where(reach, kept, 0.0)
                    carry[mode, :, lanes] = (going * leap_ref[mode, :, lanes]) * carry[mode, :, lanes] + kept

        @pl.when(first_id == last_id)
        def _():
            tiles(False)

        @pl.when(first_id != last_id)
        def _():
            tiles(True)

        return unused

    lax.fori_loop(0, blocks, one, 0)
    passing_ref[0:modes, :] = jnp.sum(carry[...], axis=1)
    line = lax.broadcasted_iota(jnp.int32, (SUB, channels), 0)
    ids = jnp.where(line == 0, segment(0, limits), segment(blocks * BLOCK - 1, limits))
    passing_ref[modes : modes + SUB, :] = ids.astype(F32)


def conv_kernel(
    bounds, signal_ref, ends_ref, near_ref, far_ref, farther_ref, decay_ref, one_ref, two_ref, four_ref, onward_ref, scale_ref, taps_ref, span_ref, out_ref, state
):
    limits = [bounds[k] for k in range(3)]
    blocks, modes, _, channels = ends_ref.shape
    start_id = segment(0, limits).astype(F32)

    def ids(ref):
        return ref[modes : modes + 1, :], ref[modes + 1 : modes + 2, :]

    near_first, near_last = ids(near_ref)
    far_first, far_last = ids(far_ref)
    _, farther_last = ids(farther_ref)
    through_far = jnp.where((far_first == far_last) & (far_first == farther_last), 1.0, 0.0)
    through_near = jnp.where((near_first == near_last) & (near_first == far_last), 1.0, 0.0)
    entering = jnp.where(near_last == start_id, 1.0, 0.0)
    span = span_ref[...]
    inside = far_ref[0:modes, :] + through_far * span * farther_ref[0:modes, :]
    inside = near_ref[0:modes, :] + through_near * span * inside
    inside = entering * inside
    for mode in range(modes):
        state[mode] = jnp.broadcast_to(inside[mode : mode + 1], (SUB, channels))

    rank = lax.broadcasted_iota(jnp.int32, (SUB, LANES), 0)

    def one(block, unused):
        begin = block * BLOCK
        last_id = segment(begin + BLOCK - 1, limits)
        before_id = segment(jnp.maximum(begin - 1, 0), limits)
        edge = segment(begin + rank * STEPS + STEPS - 1, limits)
        single = before_id == last_id

        def tiles(masked):
            if masked:
                one_in = jnp.where((rank >= 1) & (edge == pltpu.roll(edge, 1, 0)), 1.0, 0.0)
                two_in = jnp.where((rank >= 2) & (edge == pltpu.roll(edge, 2, 0)), 1.0, 0.0)
                four_in = jnp.where((rank >= 4) & (edge == pltpu.roll(edge, 4, 0)), 1.0, 0.0)
                start_in = jnp.where(edge == before_id, 1.0, 0.0)
                prior = jnp.where(rank == 0, before_id, pltpu.roll(edge, 1, 0))
                own = [segment(begin + rank * STEPS + t, limits) for t in range(STEPS)]
                open_in = [jnp.where(o == prior, 1.0, 0.0) for o in own]
            for tile in range(channels // LANES):
                lanes = pl.ds(tile * LANES, LANES)
                rows = [signal_ref[tile, pl.ds(begin + t, SUB, stride=STEPS), :] for t in range(STEPS)]
                local = []
                for t in range(STEPS):
                    total = taps_ref[0, :, lanes] * rows[t]
                    for u in range(t):
                        term = taps_ref[t - u, :, lanes] * rows[u]
                        if masked:
                            term = jnp.where(own[t] == own[u], term, 0.0)
                        total = total + term
                    local.append(total)
                carried = [None] * STEPS
                for mode in range(modes):
                    scan = ends_ref[block, mode, :, lanes]
                    moved = one_ref[mode, :, lanes] * pltpu.roll(scan, 1, 0)
                    scan = scan + (moved * one_in if masked else moved)
                    moved = two_ref[mode, :, lanes] * pltpu.roll(scan, 2, 0)
                    scan = scan + (moved * two_in if masked else moved)
                    moved = four_ref[mode, :, lanes] * pltpu.roll(scan, 4, 0)
                    scan = scan + (moved * four_in if masked else moved)
                    entry = state[mode, :, lanes]
                    moved = onward_ref[mode, :, lanes] * entry
                    scan = scan + (moved * start_in if masked else moved)
                    state[mode, :, lanes] = jnp.broadcast_to(scan[SUB - 1 : SUB], (SUB, LANES))
                    running = jnp.where(rank == 0, entry, pltpu.roll(scan, 1, 0)) * scale_ref[mode, :, lanes]
                    decay = decay_ref[mode, :, lanes]
                    for t in range(STEPS):
                        running = running * decay
                        carried[t] = running if carried[t] is None else carried[t] + running
                for t in range(STEPS):
                    more = carried[t] * open_in[t] if masked else carried[t]
                    out_ref[tile, pl.ds(begin + t, SUB, stride=STEPS), :] = local[t] + more

        @pl.when(single)
        def _():
            tiles(False)

        @pl.when(jnp.logical_not(single))
        def _():
            tiles(True)

        return unused

    lax.fori_loop(0, blocks, one, 0)


def mix_kernel(chips, starts_ref, arrived_ref, filtered_ref, out_ref, starts, landed, held, ready, table_sem, in_sems, out_sems):
    tiles, length, _ = filtered_ref.shape
    pieces = in_sems.shape[0]
    sources = arrived_ref.shape[0]
    per = sources // pieces

    def load(piece):
        slots = pl.ds(chips.index(piece) * per, per)
        return pltpu.make_async_copy(arrived_ref.at[slots], landed.at[slots], in_sems.at[piece])

    def store(block):
        rows = pl.ds(pl.multiple_of(block * BLOCK, BLOCK), BLOCK)
        return pltpu.make_async_copy(ready.at[rows, :], out_ref.at[rows, :], out_sems.at[block])

    def finish(block, unused):
        rows = pl.ds(pl.multiple_of(block * BLOCK, BLOCK), BLOCK)
        for tile in range(tiles):
            ready[rows, pl.ds(tile * LANES, LANES)] = (held[tile, rows, :] * filtered_ref[tile, rows, :]).astype(BF16)
        store(block).start()
        return unused

    table = pltpu.make_async_copy(starts_ref, starts, table_sem)
    table.start()
    for piece in range(pieces):
        load(piece).start()
    table.wait()
    complete = 0
    for piece in range(pieces):
        load(piece).wait()
        compact(chips, starts, landed, held, piece, piece + 1)
        reached = starts[(piece + 1) * per] >> 7
        lax.fori_loop(complete, reached, finish, 0)
        complete = reached
    for block in range(length // BLOCK):
        store(block).wait()


def near_by(array):
    return pltpu.with_memory_space_constraint(array, pltpu.VMEM)


def far_off(array):
    return pltpu.with_memory_space_constraint(array, pltpu.HBM)


def local_call(kernel, outs, scalars, arrays, scratch):
    spaces = (pltpu.SMEM,) * len(scalars) + (pltpu.VMEM,) * len(arrays)
    return pl.pallas_call(
        kernel,
        out_shape=outs,
        in_specs=[pl.BlockSpec(memory_space=space) for space in spaces],
        out_specs=jax.tree.map(lambda _: pl.BlockSpec(memory_space=pltpu.VMEM), outs),
        scratch_shapes=scratch,
        compiler_params=pltpu.CompilerParams(vmem_limit_bytes=24 << 20),
    )(*scalars, *[near_by(array) for array in arrays])


def passed_along(value, axis, steps):
    count = lax.axis_size(axis)
    return lax.ppermute(value, axis, [(source, source + steps) for source in range(count - steps)])


def shards(streams, load_counts, seg_ids, rates, residues, skip):
    capacity = streams.shape[0]
    groups = lax.axis_size("ch")
    channels, modes = rates.shape
    length = seg_ids.shape[0]
    blocks = length // BLOCK
    counts = load_counts[0]
    planes = jnp.transpose(streams, (1, 0, 2))
    signal_in = exchange(send((1, 2), planes, groups, channels, SIGNAL_CHIPS), SIGNAL_CHIPS)
    query_out = send((0,), planes, groups, channels, QUERY_CHIPS)

    ending = jnp.sum(jnp.where(jnp.arange(groups)[:, None] >= jnp.arange(groups)[None, :], counts[None, :], 0), axis=1)
    starts = jnp.concatenate([jnp.zeros((1,), jnp.int32), ending, jnp.zeros((BLOCK - 1 - groups,), jnp.int32)])
    starts = starts.astype(jnp.int32)
    bounds = jnp.sum((seg_ids[None, :] < jnp.arange(1, 4, dtype=jnp.int32)[:, None]).astype(jnp.int32), axis=1)

    rate = jnp.transpose(rates)
    gain = jnp.sqrt(-jnp.expm1(-2.0 * rate))
    scale = jnp.transpose(residues) * gain
    rank = jnp.arange(SUB, dtype=F32)[None, :, None]

    def power(exponent):
        return jnp.exp(-exponent * rate[:, None, :])

    flat = jnp.zeros((1, SUB, 1), F32)
    decay = power(1.0 + flat)
    weight = power((SUB - 1.0 - rank) * STEPS)
    leap = power(float(BLOCK) + flat)
    one_coef = jnp.where(rank >= 1, power(1.0 * STEPS + flat), 0.0)
    two_coef = jnp.where(rank >= 2, power(2.0 * STEPS + flat), 0.0)
    four_coef = jnp.where(rank >= 4, power(4.0 * STEPS + flat), 0.0)
    onward = power((rank + 1.0) * STEPS)
    scale_b = jnp.broadcast_to(scale[:, None, :], (modes, SUB, channels))
    lag = jnp.arange(STEPS, dtype=F32)[:, None, None]
    taps = jnp.sum(scale[None] * jnp.exp(-lag * rate[None]), axis=1)
    taps = taps + jnp.where(jnp.arange(STEPS)[:, None] == 0, skip[None, :], 0.0)
    taps_b = jnp.broadcast_to(taps[:, None, :], (STEPS, SUB, channels))
    span = jnp.exp(-float(length) * rate)

    prepared = (starts, bounds, decay, weight, leap, one_coef, two_coef, four_coef, onward, scale_b, taps_b, span)
    query_out, prepared = lax.optimization_barrier((query_out, prepared))
    starts, bounds, decay, weight, leap, one_coef, two_coef, four_coef, onward, scale_b, taps_b, span = prepared
    query_in = exchange(query_out, QUERY_CHIPS)

    padded = (channels // LANES, length + capacity, LANES)
    signal, ends, passing = local_call(
        functools.partial(scan_kernel, SIGNAL_CHIPS),
        (
            pltpu.VMEM(padded, F32),
            pltpu.VMEM((blocks, modes, SUB, channels), F32),
            pltpu.VMEM((modes + SUB, channels), F32),
        ),
        (starts, bounds),
        (signal_in, decay, weight, leap),
        [pltpu.VMEM((modes, SUB, channels), F32)],
    )
    near = passed_along(passing, "ctx", 1)
    far = passed_along(passing, "ctx", 2)
    farther = passed_along(passing, "ctx", 3)

    filtered = local_call(
        conv_kernel,
        pltpu.VMEM((channels // LANES, length, LANES), F32),
        (bounds,),
        (signal, ends, near, far, farther, decay, one_coef, two_coef, four_coef, onward, scale_b, taps_b, span),
        [pltpu.VMEM((modes, SUB, channels), F32)],
    )
    pieces = len(QUERY_CHIPS)
    return pl.pallas_call(
        functools.partial(mix_kernel, QUERY_CHIPS),
        out_shape=pltpu.HBM((length, channels), BF16),
        in_specs=[pl.BlockSpec(memory_space=space) for space in (pltpu.HBM, pltpu.HBM, pltpu.VMEM)],
        out_specs=pl.BlockSpec(memory_space=pltpu.HBM),
        scratch_shapes=[
            pltpu.SMEM(starts.shape, jnp.int32),
            pltpu.VMEM((groups, capacity, channels), BF16),
            pltpu.VMEM(padded, F32),
            pltpu.VMEM((length, channels), BF16),
            pltpu.SemaphoreType.DMA,
            pltpu.SemaphoreType.DMA((pieces,)),
            pltpu.SemaphoreType.DMA((blocks,)),
        ],
        compiler_params=pltpu.CompilerParams(vmem_limit_bytes=24 << 20),
    )(far_off(starts), far_off(query_in), near_by(filtered))


def solution(mesh):
    return jax.shard_map(
        shards,
        mesh=mesh,
        in_specs=(
            P(("ctx", "ch"), None, None),
            P("ctx", None),
            P("ctx"),
            P("ch", None),
            P("ch", None),
            P("ch"),
        ),
        out_specs=P("ctx", "ch"),
        check_vma=False,
    )
```

```python
import functools

import jax
import jax.numpy as jnp
from jax import lax
from jax.experimental import pallas as pl
from jax.experimental.pallas import tpu as pltpu
from jax.sharding import PartitionSpec as P

BLOCK = 128
STEPS = 16
LANES = 128
SUB = 8
SIGNAL_CHIPS = (10, 11, 12, 13, 14, 15, 0, 1, 2, 3, 4, 5, 6, 7, 8, 9)
QUERY_CHIPS = (10, 11, 14, 15, 12, 9, 13, 1, 7, 3, 0, 5, 2, 4, 8, 6)
LOADS = 4
F32 = jnp.float32
BF16 = jnp.bfloat16


def send_kernel(planes, chips, streams_ref, out_ref, *scratch):
    held, ready, in_sems, out_sems = scratch[:-3], scratch[-3], scratch[-2], scratch[-1]
    groups, _, channels = out_ref.shape
    width = groups * channels // LOADS
    per = groups // len(chips)
    each = len(chips) // LOADS

    def load(plane, piece):
        columns = pl.ds(piece * width, width)
        return pltpu.make_async_copy(
            streams_ref.at[planes[plane], :, columns], held[plane].at[:, columns], in_sems.at[plane, piece]
        )

    runs = []
    for piece in range(len(chips)):
        joined = piece % 2 == 1 and chips.index(piece) == chips.index(piece - 1) + 1
        runs = runs[:-1] + [(piece - 1, 2)] if joined else runs + [(piece, 1)]

    def store(run):
        piece, count = runs[run]
        goes = pl.ds(chips.index(piece) * per, count * per)
        return pltpu.make_async_copy(ready.at[pl.ds(piece * per, count * per)], out_ref.at[goes], out_sems.at[run])

    for piece in range(LOADS):
        for plane in range(len(planes)):
            load(plane, piece).start()
    for piece in range(len(chips)):
        if piece % each == 0:
            for plane in range(len(planes)):
                load(plane, piece // each).wait()
        for part in range(piece * per, (piece + 1) * per):
            columns = pl.ds(part * channels, channels)
            value = held[0][:, columns]
            for other in held[1:]:
                value = value * other[:, columns]
            ready[part] = value
        for run, (begin, count) in enumerate(runs):
            if begin + count == piece + 1:
                store(run).start()
    for run in range(len(runs)):
        store(run).wait()


def send(planes, streams, groups, channels, chips):
    rows = streams.shape[1]
    return pl.pallas_call(
        functools.partial(send_kernel, planes, chips),
        out_shape=pltpu.HBM((groups, rows, channels), BF16),
        in_specs=[pl.BlockSpec(memory_space=pltpu.HBM)],
        out_specs=pl.BlockSpec(memory_space=pltpu.HBM),
        scratch_shapes=[pltpu.VMEM((rows, groups * channels), BF16) for _ in planes]
        + [
            pltpu.VMEM((groups, rows, channels), BF16),
            pltpu.SemaphoreType.DMA((len(planes), LOADS)),
            pltpu.SemaphoreType.DMA((len(chips),)),
        ],
        compiler_params=pltpu.CompilerParams(vmem_limit_bytes=24 << 20),
    )(far_off(streams))


def exchange(value, chips):
    per = value.shape[0] // len(chips)
    order = [chip * per + core for chip in chips for core in range(per)]
    return lax.all_to_all(value, "ch", split_axis=0, concat_axis=0, axis_index_groups=[order], tiled=True)


def compact(chips, starts, arrived_ref, into_ref, first, last):
    groups, rows, channels = arrived_ref.shape
    per = groups // len(chips)
    for chip in range(first, last):
        slots = chips.index(chip) * per

        def place(core, unused, chip=chip, slots=slots):
            begin = starts[chip * per + core]
            for part in range(0, rows, 2 * SUB):
                for tile in range(channels // LANES):
                    piece = arrived_ref[slots + core, pl.ds(part, 2 * SUB), pl.ds(tile * LANES, LANES)].astype(F32)
                    into_ref[tile, pl.ds(begin + part, SUB), :] = piece[:SUB]
                    into_ref[tile, pl.ds(begin + part + SUB, SUB), :] = piece[SUB:]
            return unused

        lax.fori_loop(0, per, place, 0)


def segment(position, bounds):
    total = (position >= bounds[0]).astype(jnp.int32)
    for bound in bounds[1:]:
        total = total + (position >= bound).astype(jnp.int32)
    return total


def scan_kernel(chips, starts, bounds, arrived_ref, decay_ref, weight_ref, leap_ref, signal_ref, ends_ref, passing_ref, carry):
    limits = [bounds[k] for k in range(3)]
    blocks, modes, _, channels = ends_ref.shape
    carry[...] = jnp.zeros_like(carry)
    rank = lax.broadcasted_iota(jnp.int32, (SUB, LANES), 0)
    compact(chips, starts, arrived_ref, signal_ref, 0, len(chips))

    def one(block, unused):
        begin = block * BLOCK
        first_id = segment(begin, limits)
        last_id = segment(begin + BLOCK - 1, limits)
        before_id = segment(begin - 1, limits)
        reach = segment(begin + rank * STEPS + STEPS - 1, limits) == last_id
        going = jnp.where(before_id == last_id, 1.0, 0.0)

        def tiles(masked):
            if masked:
                own = [segment(begin + rank * STEPS + t, limits) for t in range(STEPS)]
            for tile in range(channels // LANES):
                lanes = pl.ds(tile * LANES, LANES)
                rows = [signal_ref[tile, pl.ds(begin + t, SUB, stride=STEPS), :] for t in range(STEPS)]
                if masked:
                    rows = [jnp.where(o == own[-1], r, 0.0) for o, r in zip(own, rows)]
                for mode in range(modes):
                    decay = decay_ref[mode, :, lanes]
                    state = rows[0]
                    for t in range(1, STEPS):
                        state = decay * state + rows[t]
                    ends_ref[block, mode, :, lanes] = state
                    kept = weight_ref[mode, :, lanes] * state
                    if masked:
                        kept = jnp.where(reach, kept, 0.0)
                    carry[mode, :, lanes] = (going * leap_ref[mode, :, lanes]) * carry[mode, :, lanes] + kept

        @pl.when(first_id == last_id)
        def _():
            tiles(False)

        @pl.when(first_id != last_id)
        def _():
            tiles(True)

        return unused

    lax.fori_loop(0, blocks, one, 0)
    passing_ref[0:modes, :] = jnp.sum(carry[...], axis=1)
    line = lax.broadcasted_iota(jnp.int32, (SUB, channels), 0)
    ids = jnp.where(line == 0, segment(0, limits), segment(blocks * BLOCK - 1, limits))
    passing_ref[modes : modes + SUB, :] = ids.astype(F32)


def conv_kernel(
    bounds, signal_ref, ends_ref, near_ref, far_ref, farther_ref, decay_ref, one_ref, two_ref, four_ref, onward_ref, scale_ref, taps_ref, span_ref, out_ref, state
):
    limits = [bounds[k] for k in range(3)]
    blocks, modes, _, channels = ends_ref.shape
    start_id = segment(0, limits).astype(F32)

    def ids(ref):
        return ref[modes : modes + 1, :], ref[modes + 1 : modes + 2, :]

    near_first, near_last = ids(near_ref)
    far_first, far_last = ids(far_ref)
    _, farther_last = ids(farther_ref)
    through_far = jnp.where((far_first == far_last) & (far_first == farther_last), 1.0, 0.0)
    through_near = jnp.where((near_first == near_last) & (near_first == far_last), 1.0, 0.0)
    entering = jnp.where(near_last == start_id, 1.0, 0.0)
    span = span_ref[...]
    inside = far_ref[0:modes, :] + through_far * span * farther_ref[0:modes, :]
    inside = near_ref[0:modes, :] + through_near * span * inside
    inside = entering * inside
    for mode in range(modes):
        state[mode] = jnp.broadcast_to(inside[mode : mode + 1], (SUB, channels))

    rank = lax.broadcasted_iota(jnp.int32, (SUB, LANES), 0)

    def one(block, unused):
        begin = block * BLOCK
        last_id = segment(begin + BLOCK - 1, limits)
        before_id = segment(jnp.maximum(begin - 1, 0), limits)
        edge = segment(begin + rank * STEPS + STEPS - 1, limits)
        single = before_id == last_id

        def tiles(masked):
            if masked:
                one_in = jnp.where((rank >= 1) & (edge == pltpu.roll(edge, 1, 0)), 1.0, 0.0)
                two_in = jnp.where((rank >= 2) & (edge == pltpu.roll(edge, 2, 0)), 1.0, 0.0)
                four_in = jnp.where((rank >= 4) & (edge == pltpu.roll(edge, 4, 0)), 1.0, 0.0)
                start_in = jnp.where(edge == before_id, 1.0, 0.0)
                prior = jnp.where(rank == 0, before_id, pltpu.roll(edge, 1, 0))
                own = [segment(begin + rank * STEPS + t, limits) for t in range(STEPS)]
                open_in = [jnp.where(o == prior, 1.0, 0.0) for o in own]
            for tile in range(channels // LANES):
                lanes = pl.ds(tile * LANES, LANES)
                rows = [signal_ref[tile, pl.ds(begin + t, SUB, stride=STEPS), :] for t in range(STEPS)]
                local = []
                for t in range(STEPS):
                    total = taps_ref[0, :, lanes] * rows[t]
                    for u in range(t):
                        term = taps_ref[t - u, :, lanes] * rows[u]
                        if masked:
                            term = jnp.where(own[t] == own[u], term, 0.0)
                        total = total + term
                    local.append(total)
                carried = [None] * STEPS
                for mode in range(modes):
                    scan = ends_ref[block, mode, :, lanes]
                    moved = one_ref[mode, :, lanes] * pltpu.roll(scan, 1, 0)
                    scan = scan + (moved * one_in if masked else moved)
                    moved = two_ref[mode, :, lanes] * pltpu.roll(scan, 2, 0)
                    scan = scan + (moved * two_in if masked else moved)
                    moved = four_ref[mode, :, lanes] * pltpu.roll(scan, 4, 0)
                    scan = scan + (moved * four_in if masked else moved)
                    entry = state[mode, :, lanes]
                    moved = onward_ref[mode, :, lanes] * entry
                    scan = scan + (moved * start_in if masked else moved)
                    state[mode, :, lanes] = jnp.broadcast_to(scan[SUB - 1 : SUB], (SUB, LANES))
                    running = jnp.where(rank == 0, entry, pltpu.roll(scan, 1, 0)) * scale_ref[mode, :, lanes]
                    decay = decay_ref[mode, :, lanes]
                    for t in range(STEPS):
                        running = running * decay
                        carried[t] = running if carried[t] is None else carried[t] + running
                for t in range(STEPS):
                    more = carried[t] * open_in[t] if masked else carried[t]
                    out_ref[tile, pl.ds(begin + t, SUB, stride=STEPS), :] = local[t] + more

        @pl.when(single)
        def _():
            tiles(False)

        @pl.when(jnp.logical_not(single))
        def _():
            tiles(True)

        return unused

    lax.fori_loop(0, blocks, one, 0)


def mix_kernel(chips, starts_ref, arrived_ref, filtered_ref, out_ref, starts, landed, held, ready, table_sem, in_sems, out_sems):
    tiles, length, _ = filtered_ref.shape
    pieces = in_sems.shape[0]
    sources = arrived_ref.shape[0]
    per = sources // pieces

    def load(piece):
        slots = pl.ds(chips.index(piece) * per, per)
        return pltpu.make_async_copy(arrived_ref.at[slots], landed.at[slots], in_sems.at[piece])

    def store(block):
        rows = pl.ds(pl.multiple_of(block * BLOCK, BLOCK), BLOCK)
        return pltpu.make_async_copy(ready.at[rows, :], out_ref.at[rows, :], out_sems.at[block])

    def finish(block, unused):
        rows = pl.ds(pl.multiple_of(block * BLOCK, BLOCK), BLOCK)
        for tile in range(tiles):
            ready[rows, pl.ds(tile * LANES, LANES)] = (held[tile, rows, :] * filtered_ref[tile, rows, :]).astype(BF16)
        store(block).start()
        return unused

    table = pltpu.make_async_copy(starts_ref, starts, table_sem)
    table.start()
    for piece in range(pieces):
        load(piece).start()
    table.wait()
    complete = 0
    for piece in range(pieces):
        load(piece).wait()
        compact(chips, starts, landed, held, piece, piece + 1)
        reached = starts[(piece + 1) * per] >> 7
        lax.fori_loop(complete, reached, finish, 0)
        complete = reached
    for block in range(length // BLOCK):
        store(block).wait()


def near_by(array):
    return pltpu.with_memory_space_constraint(array, pltpu.VMEM)


def far_off(array):
    return pltpu.with_memory_space_constraint(array, pltpu.HBM)


def local_call(kernel, outs, scalars, arrays, scratch):
    spaces = (pltpu.SMEM,) * len(scalars) + (pltpu.VMEM,) * len(arrays)
    return pl.pallas_call(
        kernel,
        out_shape=outs,
        in_specs=[pl.BlockSpec(memory_space=space) for space in spaces],
        out_specs=jax.tree.map(lambda _: pl.BlockSpec(memory_space=pltpu.VMEM), outs),
        scratch_shapes=scratch,
        compiler_params=pltpu.CompilerParams(vmem_limit_bytes=24 << 20),
    )(*scalars, *[near_by(array) for array in arrays])


def passed_along(value, axis, steps):
    count = lax.axis_size(axis)
    return lax.ppermute(value, axis, [(source, source + steps) for source in range(count - steps)])


def shards(streams, load_counts, seg_ids, rates, residues, skip):
    capacity = streams.shape[0]
    groups = lax.axis_size("ch")
    channels, modes = rates.shape
    length = seg_ids.shape[0]
    blocks = length // BLOCK
    counts = load_counts[0]
    planes = jnp.transpose(streams, (1, 0, 2))
    signal_in = exchange(send((1, 2), planes, groups, channels, SIGNAL_CHIPS), SIGNAL_CHIPS)
    query_out = send((0,), planes, groups, channels, QUERY_CHIPS)

    ending = jnp.sum(jnp.where(jnp.arange(groups)[:, None] >= jnp.arange(groups)[None, :], counts[None, :], 0), axis=1)
    starts = jnp.concatenate([jnp.zeros((1,), jnp.int32), ending, jnp.zeros((BLOCK - 1 - groups,), jnp.int32)])
    starts = starts.astype(jnp.int32)
    bounds = jnp.sum((seg_ids[None, :] < jnp.arange(1, 4, dtype=jnp.int32)[:, None]).astype(jnp.int32), axis=1)

    rate = jnp.transpose(rates)
    gain = jnp.sqrt(-jnp.expm1(-2.0 * rate))
    scale = jnp.transpose(residues) * gain
    rank = jnp.arange(SUB, dtype=F32)[None, :, None]

    def power(exponent):
        return jnp.exp(-exponent * rate[:, None, :])

    flat = jnp.zeros((1, SUB, 1), F32)
    decay = power(1.0 + flat)
    weight = power((SUB - 1.0 - rank) * STEPS)
    leap = power(float(BLOCK) + flat)
    one_coef = jnp.where(rank >= 1, power(1.0 * STEPS + flat), 0.0)
    two_coef = jnp.where(rank >= 2, power(2.0 * STEPS + flat), 0.0)
    four_coef = jnp.where(rank >= 4, power(4.0 * STEPS + flat), 0.0)
    onward = power((rank + 1.0) * STEPS)
    scale_b = jnp.broadcast_to(scale[:, None, :], (modes, SUB, channels))
    lag = jnp.arange(STEPS, dtype=F32)[:, None, None]
    taps = jnp.sum(scale[None] * jnp.exp(-lag * rate[None]), axis=1)
    taps = taps + jnp.where(jnp.arange(STEPS)[:, None] == 0, skip[None, :], 0.0)
    taps_b = jnp.broadcast_to(taps[:, None, :], (STEPS, SUB, channels))
    span = jnp.exp(-float(length) * rate)

    prepared = (starts, bounds, decay, weight, leap, one_coef, two_coef, four_coef, onward, scale_b, taps_b, span)
    query_out, prepared = lax.optimization_barrier((query_out, prepared))
    starts, bounds, decay, weight, leap, one_coef, two_coef, four_coef, onward, scale_b, taps_b, span = prepared
    query_in = exchange(query_out, QUERY_CHIPS)

    padded = (channels // LANES, length + capacity, LANES)
    signal, ends, passing = local_call(
        functools.partial(scan_kernel, SIGNAL_CHIPS),
        (
            pltpu.VMEM(padded, F32),
            pltpu.VMEM((blocks, modes, SUB, channels), F32),
            pltpu.VMEM((modes + SUB, channels), F32),
        ),
        (starts, bounds),
        (signal_in, decay, weight, leap),
        [pltpu.VMEM((modes, SUB, channels), F32)],
    )
    near = passed_along(passing, "ctx", 1)
    far = passed_along(passing, "ctx", 2)
    farther = passed_along(passing, "ctx", 3)

    filtered = local_call(
        conv_kernel,
        pltpu.VMEM((channels // LANES, length, LANES), F32),
        (bounds,),
        (signal, ends, near, far, farther, decay, one_coef, two_coef, four_coef, onward, scale_b, taps_b, span),
        [pltpu.VMEM((modes, SUB, channels), F32)],
    )
    pieces = len(QUERY_CHIPS)
    return pl.pallas_call(
        functools.partial(mix_kernel, QUERY_CHIPS),
        out_shape=pltpu.HBM((length, channels), BF16),
        in_specs=[pl.BlockSpec(memory_space=space) for space in (pltpu.HBM, pltpu.HBM, pltpu.VMEM)],
        out_specs=pl.BlockSpec(memory_space=pltpu.HBM),
        scratch_shapes=[
            pltpu.SMEM(starts.shape, jnp.int32),
            pltpu.VMEM((groups, capacity, channels), BF16),
            pltpu.VMEM(padded, F32),
            pltpu.VMEM((length, channels), BF16),
            pltpu.SemaphoreType.DMA,
            pltpu.SemaphoreType.DMA((pieces,)),
            pltpu.SemaphoreType.DMA((blocks,)),
        ],
        compiler_params=pltpu.CompilerParams(vmem_limit_bytes=24 << 20),
    )(far_off(starts), far_off(query_in), near_by(filtered))


def solution(mesh):
    return jax.shard_map(
        shards,
        mesh=mesh,
        in_specs=(
            P(("ctx", "ch"), None, None),
            P("ctx", None),
            P("ctx"),
            P("ch", None),
            P("ch", None),
            P("ch"),
        ),
        out_specs=P("ctx", "ch"),
        check_vma=False,
    )
```

```python
import functools

import jax
import jax.numpy as jnp
from jax import lax
from jax.experimental import pallas as pl
from jax.experimental.pallas import tpu as pltpu
from jax.sharding import PartitionSpec as P

BLOCK = 128
STEPS = 16
LANES = 128
SUB = 8
SIGNAL_CHIPS = (10, 11, 12, 13, 14, 15, 0, 1, 2, 3, 4, 5, 6, 7, 8, 9)
QUERY_CHIPS = (10, 11, 14, 15, 12, 9, 13, 1, 7, 3, 0, 5, 2, 4, 8, 6)
LOADS = 4
F32 = jnp.float32
BF16 = jnp.bfloat16


def send_kernel(planes, chips, streams_ref, out_ref, *scratch):
    held, ready, in_sems, out_sems = scratch[:-3], scratch[-3], scratch[-2], scratch[-1]
    groups, _, channels = out_ref.shape
    width = groups * channels // LOADS
    per = groups // len(chips)
    each = len(chips) // LOADS

    def load(plane, piece):
        columns = pl.ds(piece * width, width)
        return pltpu.make_async_copy(
            streams_ref.at[planes[plane], :, columns], held[plane].at[:, columns], in_sems.at[plane, piece]
        )

    runs = []
    for piece in range(len(chips)):
        joined = piece % 2 == 1 and chips.index(piece) == chips.index(piece - 1) + 1
        runs = runs[:-1] + [(piece - 1, 2)] if joined else runs + [(piece, 1)]

    def store(run):
        piece, count = runs[run]
        goes = pl.ds(chips.index(piece) * per, count * per)
        return pltpu.make_async_copy(ready.at[pl.ds(piece * per, count * per)], out_ref.at[goes], out_sems.at[run])

    for piece in range(LOADS):
        for plane in range(len(planes)):
            load(plane, piece).start()
    for piece in range(len(chips)):
        if piece % each == 0:
            for plane in range(len(planes)):
                load(plane, piece // each).wait()
        for part in range(piece * per, (piece + 1) * per):
            columns = pl.ds(part * channels, channels)
            value = held[0][:, columns]
            for other in held[1:]:
                value = value * other[:, columns]
            ready[part] = value
        for run, (begin, count) in enumerate(runs):
            if begin + count == piece + 1:
                store(run).start()
    for run in range(len(runs)):
        store(run).wait()


def send(planes, streams, groups, channels, chips):
    rows = streams.shape[1]
    return pl.pallas_call(
        functools.partial(send_kernel, planes, chips),
        out_shape=pltpu.HBM((groups, rows, channels), BF16),
        in_specs=[pl.BlockSpec(memory_space=pltpu.HBM)],
        out_specs=pl.BlockSpec(memory_space=pltpu.HBM),
        scratch_shapes=[pltpu.VMEM((rows, groups * channels), BF16) for _ in planes]
        + [
            pltpu.VMEM((groups, rows, channels), BF16),
            pltpu.SemaphoreType.DMA((len(planes), LOADS)),
            pltpu.SemaphoreType.DMA((len(chips),)),
        ],
        compiler_params=pltpu.CompilerParams(vmem_limit_bytes=24 << 20),
    )(far_off(streams))


def exchange(value, chips):
    per = value.shape[0] // len(chips)
    order = [chip * per + core for chip in chips for core in range(per)]
    return lax.all_to_all(value, "ch", split_axis=0, concat_axis=0, axis_index_groups=[order], tiled=True)


def compact(chips, starts, arrived_ref, into_ref, first, last):
    groups, rows, channels = arrived_ref.shape
    per = groups // len(chips)
    for chip in range(first, last):
        slots = chips.index(chip) * per

        def place(core, unused, chip=chip, slots=slots):
            begin = starts[chip * per + core]
            for part in range(0, rows, 2 * SUB):
                for tile in range(channels // LANES):
                    piece = arrived_ref[slots + core, pl.ds(part, 2 * SUB), pl.ds(tile * LANES, LANES)].astype(F32)
                    into_ref[tile, pl.ds(begin + part, SUB), :] = piece[:SUB]
                    into_ref[tile, pl.ds(begin + part + SUB, SUB), :] = piece[SUB:]
            return unused

        lax.fori_loop(0, per, place, 0)


def segment(position, bounds):
    total = (position >= bounds[0]).astype(jnp.int32)
    for bound in bounds[1:]:
        total = total + (position >= bound).astype(jnp.int32)
    return total


def scan_kernel(chips, starts, bounds, arrived_ref, decay_ref, weight_ref, leap_ref, signal_ref, ends_ref, passing_ref, carry):
    limits = [bounds[k] for k in range(3)]
    blocks, modes, _, channels = ends_ref.shape
    carry[...] = jnp.zeros_like(carry)
    rank = lax.broadcasted_iota(jnp.int32, (SUB, LANES), 0)
    compact(chips, starts, arrived_ref, signal_ref, 0, len(chips))

    def one(block, unused):
        begin = block * BLOCK
        first_id = segment(begin, limits)
        last_id = segment(begin + BLOCK - 1, limits)
        before_id = segment(begin - 1, limits)
        reach = segment(begin + rank * STEPS + STEPS - 1, limits) == last_id
        going = jnp.where(before_id == last_id, 1.0, 0.0)

        def tiles(masked):
            if masked:
                own = [segment(begin + rank * STEPS + t, limits) for t in range(STEPS)]
            for tile in range(channels // LANES):
                lanes = pl.ds(tile * LANES, LANES)
                rows = [signal_ref[tile, pl.ds(begin + t, SUB, stride=STEPS), :] for t in range(STEPS)]
                if masked:
                    rows = [jnp.where(o == own[-1], r, 0.0) for o, r in zip(own, rows)]
                for mode in range(modes):
                    decay = decay_ref[mode, :, lanes]
                    state = rows[0]
                    for t in range(1, STEPS):
                        state = decay * state + rows[t]
                    ends_ref[block, mode, :, lanes] = state
                    kept = weight_ref[mode, :, lanes] * state
                    if masked:
                        kept = jnp.where(reach, kept, 0.0)
                    carry[mode, :, lanes] = (going * leap_ref[mode, :, lanes]) * carry[mode, :, lanes] + kept

        @pl.when(first_id == last_id)
        def _():
            tiles(False)

        @pl.when(first_id != last_id)
        def _():
            tiles(True)

        return unused

    lax.fori_loop(0, blocks, one, 0)
    passing_ref[0:modes, :] = jnp.sum(carry[...], axis=1)
    line = lax.broadcasted_iota(jnp.int32, (SUB, channels), 0)
    ids = jnp.where(line == 0, segment(0, limits), segment(blocks * BLOCK - 1, limits))
    passing_ref[modes : modes + SUB, :] = ids.astype(F32)


def conv_kernel(
    bounds, signal_ref, ends_ref, near_ref, far_ref, farther_ref, decay_ref, one_ref, two_ref, four_ref, onward_ref, scale_ref, taps_ref, span_ref, out_ref, state
):
    limits = [bounds[k] for k in range(3)]
    blocks, modes, _, channels = ends_ref.shape
    start_id = segment(0, limits).astype(F32)

    def ids(ref):
        return ref[modes : modes + 1, :], ref[modes + 1 : modes + 2, :]

    near_first, near_last = ids(near_ref)
    far_first, far_last = ids(far_ref)
    _, farther_last = ids(farther_ref)
    through_far = jnp.where((far_first == far_last) & (far_first == farther_last), 1.0, 0.0)
    through_near = jnp.where((near_first == near_last) & (near_first == far_last), 1.0, 0.0)
    entering = jnp.where(near_last == start_id, 1.0, 0.0)
    span = span_ref[...]
    inside = far_ref[0:modes, :] + through_far * span * farther_ref[0:modes, :]
    inside = near_ref[0:modes, :] + through_near * span * inside
    inside = entering * inside
    for mode in range(modes):
        state[mode] = jnp.broadcast_to(inside[mode : mode + 1], (SUB, channels))

    rank = lax.broadcasted_iota(jnp.int32, (SUB, LANES), 0)

    def one(block, unused):
        begin = block * BLOCK
        last_id = segment(begin + BLOCK - 1, limits)
        before_id = segment(jnp.maximum(begin - 1, 0), limits)
        edge = segment(begin + rank * STEPS + STEPS - 1, limits)
        single = before_id == last_id

        def tiles(masked):
            if masked:
                one_in = jnp.where((rank >= 1) & (edge == pltpu.roll(edge, 1, 0)), 1.0, 0.0)
                two_in = jnp.where((rank >= 2) & (edge == pltpu.roll(edge, 2, 0)), 1.0, 0.0)
                four_in = jnp.where((rank >= 4) & (edge == pltpu.roll(edge, 4, 0)), 1.0, 0.0)
                start_in = jnp.where(edge == before_id, 1.0, 0.0)
                prior = jnp.where(rank == 0, before_id, pltpu.roll(edge, 1, 0))
                own = [segment(begin + rank * STEPS + t, limits) for t in range(STEPS)]
                open_in = [jnp.where(o == prior, 1.0, 0.0) for o in own]
            for tile in range(channels // LANES):
                lanes = pl.ds(tile * LANES, LANES)
                rows = [signal_ref[tile, pl.ds(begin + t, SUB, stride=STEPS), :] for t in range(STEPS)]
                local = []
                for t in range(STEPS):
                    total = taps_ref[0, :, lanes] * rows[t]
                    for u in range(t):
                        term = taps_ref[t - u, :, lanes] * rows[u]
                        if masked:
                            term = jnp.where(own[t] == own[u], term, 0.0)
                        total = total + term
                    local.append(total)
                carried = [None] * STEPS
                for mode in range(modes):
                    scan = ends_ref[block, mode, :, lanes]
                    moved = one_ref[mode, :, lanes] * pltpu.roll(scan, 1, 0)
                    scan = scan + (moved * one_in if masked else moved)
                    moved = two_ref[mode, :, lanes] * pltpu.roll(scan, 2, 0)
                    scan = scan + (moved * two_in if masked else moved)
                    moved = four_ref[mode, :, lanes] * pltpu.roll(scan, 4, 0)
                    scan = scan + (moved * four_in if masked else moved)
                    entry = state[mode, :, lanes]
                    moved = onward_ref[mode, :, lanes] * entry
                    scan = scan + (moved * start_in if masked else moved)
                    state[mode, :, lanes] = jnp.broadcast_to(scan[SUB - 1 : SUB], (SUB, LANES))
                    running = jnp.where(rank == 0, entry, pltpu.roll(scan, 1, 0)) * scale_ref[mode, :, lanes]
                    decay = decay_ref[mode, :, lanes]
                    for t in range(STEPS):
                        running = running * decay
                        carried[t] = running if carried[t] is None else carried[t] + running
                for t in range(STEPS):
                    more = carried[t] * open_in[t] if masked else carried[t]
                    out_ref[tile, pl.ds(begin + t, SUB, stride=STEPS), :] = local[t] + more

        @pl.when(single)
        def _():
            tiles(False)

        @pl.when(jnp.logical_not(single))
        def _():
            tiles(True)

        return unused

    lax.fori_loop(0, blocks, one, 0)


def mix_kernel(chips, starts_ref, arrived_ref, filtered_ref, out_ref, starts, landed, held, ready, table_sem, in_sems, out_sems):
    tiles, length, _ = filtered_ref.shape
    pieces = in_sems.shape[0]
    sources = arrived_ref.shape[0]
    per = sources // pieces

    def load(piece):
        joined = piece + 1 < pieces and piece % 2 == 0 and chips.index(piece + 1) == chips.index(piece) + 1
        slots = pl.ds(chips.index(piece) * per, per * (2 if joined else 1))
        return pltpu.make_async_copy(arrived_ref.at[slots], landed.at[slots], in_sems.at[piece])

    def store(block):
        rows = pl.ds(pl.multiple_of(block * BLOCK, BLOCK), BLOCK)
        return pltpu.make_async_copy(ready.at[rows, :], out_ref.at[rows, :], out_sems.at[block])

    def finish(block, unused):
        rows = pl.ds(pl.multiple_of(block * BLOCK, BLOCK), BLOCK)
        for tile in range(tiles):
            ready[rows, pl.ds(tile * LANES, LANES)] = (held[tile, rows, :] * filtered_ref[tile, rows, :]).astype(BF16)
        store(block).start()
        return unused

    table = pltpu.make_async_copy(starts_ref, starts, table_sem)
    table.start()
    heads = [p for p in range(pieces) if p % 2 == 0 or chips.index(p) != chips.index(p - 1) + 1]
    for piece in heads:
        load(piece).start()
    table.wait()
    complete = 0
    for piece in range(pieces):
        if piece in heads:
            load(piece).wait()
        compact(chips, starts, landed, held, piece, piece + 1)
        reached = starts[(piece + 1) * per] >> 7
        lax.fori_loop(complete, reached, finish, 0)
        complete = reached
    for block in range(length // BLOCK):
        store(block).wait()


def near_by(array):
    return pltpu.with_memory_space_constraint(array, pltpu.VMEM)


def far_off(array):
    return pltpu.with_memory_space_constraint(array, pltpu.HBM)


def local_call(kernel, outs, scalars, arrays, scratch):
    spaces = (pltpu.SMEM,) * len(scalars) + (pltpu.VMEM,) * len(arrays)
    return pl.pallas_call(
        kernel,
        out_shape=outs,
        in_specs=[pl.BlockSpec(memory_space=space) for space in spaces],
        out_specs=jax.tree.map(lambda _: pl.BlockSpec(memory_space=pltpu.VMEM), outs),
        scratch_shapes=scratch,
        compiler_params=pltpu.CompilerParams(vmem_limit_bytes=24 << 20),
    )(*scalars, *[near_by(array) for array in arrays])


def passed_along(value, axis, steps):
    count = lax.axis_size(axis)
    return lax.ppermute(value, axis, [(source, source + steps) for source in range(count - steps)])


def shards(streams, load_counts, seg_ids, rates, residues, skip):
    capacity = streams.shape[0]
    groups = lax.axis_size("ch")
    channels, modes = rates.shape
    length = seg_ids.shape[0]
    blocks = length // BLOCK
    counts = load_counts[0]
    planes = jnp.transpose(streams, (1, 0, 2))
    signal_in = exchange(send((1, 2), planes, groups, channels, SIGNAL_CHIPS), SIGNAL_CHIPS)
    query_out = send((0,), planes, groups, channels, QUERY_CHIPS)

    ending = jnp.sum(jnp.where(jnp.arange(groups)[:, None] >= jnp.arange(groups)[None, :], counts[None, :], 0), axis=1)
    starts = jnp.concatenate([jnp.zeros((1,), jnp.int32), ending, jnp.zeros((BLOCK - 1 - groups,), jnp.int32)])
    starts = starts.astype(jnp.int32)
    bounds = jnp.sum((seg_ids[None, :] < jnp.arange(1, 4, dtype=jnp.int32)[:, None]).astype(jnp.int32), axis=1)

    rate = jnp.transpose(rates)
    gain = jnp.sqrt(-jnp.expm1(-2.0 * rate))
    scale = jnp.transpose(residues) * gain
    rank = jnp.arange(SUB, dtype=F32)[None, :, None]

    def power(exponent):
        return jnp.exp(-exponent * rate[:, None, :])

    flat = jnp.zeros((1, SUB, 1), F32)
    decay = power(1.0 + flat)
    weight = power((SUB - 1.0 - rank) * STEPS)
    leap = power(float(BLOCK) + flat)
    one_coef = jnp.where(rank >= 1, power(1.0 * STEPS + flat), 0.0)
    two_coef = jnp.where(rank >= 2, power(2.0 * STEPS + flat), 0.0)
    four_coef = jnp.where(rank >= 4, power(4.0 * STEPS + flat), 0.0)
    onward = power((rank + 1.0) * STEPS)
    scale_b = jnp.broadcast_to(scale[:, None, :], (modes, SUB, channels))
    lag = jnp.arange(STEPS, dtype=F32)[:, None, None]
    taps = jnp.sum(scale[None] * jnp.exp(-lag * rate[None]), axis=1)
    taps = taps + jnp.where(jnp.arange(STEPS)[:, None] == 0, skip[None, :], 0.0)
    taps_b = jnp.broadcast_to(taps[:, None, :], (STEPS, SUB, channels))
    span = jnp.exp(-float(length) * rate)

    prepared = (starts, bounds, decay, weight, leap, one_coef, two_coef, four_coef, onward, scale_b, taps_b, span)
    query_out, prepared = lax.optimization_barrier((query_out, prepared))
    starts, bounds, decay, weight, leap, one_coef, two_coef, four_coef, onward, scale_b, taps_b, span = prepared
    query_in = exchange(query_out, QUERY_CHIPS)

    padded = (channels // LANES, length + capacity, LANES)
    signal, ends, passing = local_call(
        functools.partial(scan_kernel, SIGNAL_CHIPS),
        (
            pltpu.VMEM(padded, F32),
            pltpu.VMEM((blocks, modes, SUB, channels), F32),
            pltpu.VMEM((modes + SUB, channels), F32),
        ),
        (starts, bounds),
        (signal_in, decay, weight, leap),
        [pltpu.VMEM((modes, SUB, channels), F32)],
    )
    near = passed_along(passing, "ctx", 1)
    far = passed_along(passing, "ctx", 2)
    farther = passed_along(passing, "ctx", 3)

    filtered = local_call(
        conv_kernel,
        pltpu.VMEM((channels // LANES, length, LANES), F32),
        (bounds,),
        (signal, ends, near, far, farther, decay, one_coef, two_coef, four_coef, onward, scale_b, taps_b, span),
        [pltpu.VMEM((modes, SUB, channels), F32)],
    )
    pieces = len(QUERY_CHIPS)
    return pl.pallas_call(
        functools.partial(mix_kernel, QUERY_CHIPS),
        out_shape=pltpu.HBM((length, channels), BF16),
        in_specs=[pl.BlockSpec(memory_space=space) for space in (pltpu.HBM, pltpu.HBM, pltpu.VMEM)],
        out_specs=pl.BlockSpec(memory_space=pltpu.HBM),
        scratch_shapes=[
            pltpu.SMEM(starts.shape, jnp.int32),
            pltpu.VMEM((groups, capacity, channels), BF16),
            pltpu.VMEM(padded, F32),
            pltpu.VMEM((length, channels), BF16),
            pltpu.SemaphoreType.DMA,
            pltpu.SemaphoreType.DMA((pieces,)),
            pltpu.SemaphoreType.DMA((blocks,)),
        ],
        compiler_params=pltpu.CompilerParams(vmem_limit_bytes=24 << 20),
    )(far_off(starts), far_off(query_in), near_by(filtered))


def solution(mesh):
    return jax.shard_map(
        shards,
        mesh=mesh,
        in_specs=(
            P(("ctx", "ch"), None, None),
            P("ctx", None),
            P("ctx"),
            P("ch", None),
            P("ch", None),
            P("ch"),
        ),
        out_specs=P("ctx", "ch"),
        check_vma=False,
    )
```
